32 devices in a mesh: node: 8 (over z, x), mp: 4 (over y, core).
Axes of the slice: x: 2, y: 2, z: 4, core: 2. Of those that a mesh axis runs over, the one named last changes fastest.
Arguments:
- queries: bfloat16 [32, 64, 128], P('node', 'mp'), may hold values from -8 to 8
- root_keys: bfloat16 [16384, 8, 128], P('node', 'mp'), may hold values from -6 to 6
- root_values: bfloat16 [16384, 8, 128], P('node', 'mp'), may hold values from -6 to 6
- mid_keys: bfloat16 [8, 1024, 8, 128], P('node', None, 'mp'), may hold values from -6 to 6
- mid_values: bfloat16 [8, 1024, 8, 128], P('node', None, 'mp'), may hold values from -6 to 6
- leaf_keys: bfloat16 [32, 256, 8, 128], P('node', None, 'mp'), may hold values from -6 to 6
- leaf_values: bfloat16 [32, 256, 8, 128], P('node', None, 'mp'), may hold values from -6 to 6
- mid_length: int32 [8], replicated, may hold values from 1 to 1024
- leaf_length: int32 [32], P('node'), may hold values from 1 to 256
- branch_mid: int32 [32, 1], replicated, may hold values from 0 to 7; in each aligned block of 32 rows (0 to 31, 32 to 63, ...) at most 8 rows name the same one
- residual: bfloat16 [32, 8192], P(None, 'node'), may hold values from -6 to 6
- norm_gain: float32 [8192], P('node'), may hold values from 0.5 to 1.5
- out_weight: bfloat16 [8192, 8192], P('mp', 'node'), may hold values from -0.0625 to 0.0625
- gate_weight: bfloat16 [8192, 28672], P('node', 'mp'), may hold values from -0.0625 to 0.0625
- up_weight: bfloat16 [8192, 28672], P('node', 'mp'), may hold values from -0.0625 to 0.0625
- down_weight: bfloat16 [28672, 8192], P('mp', 'node'), may hold values from -0.03125 to 0.03125
Outputs:
- layer_out: bfloat16 [32, 8192], P('mp', 'node')
The draws below stay inside these ranges and needn't reach their ends.
Inputs may be any that keep to these rules, and one draw needn't show every extreme that they name: `branch_mid`: every inner tree node lies on the path of 1 to 8 branches, and some node on exactly 8.
All inputs are finite; a program needn't handle non-finite values.
Results may differ from the reference program's by a relative error of at most 0.015.
Values may be sent and summed in bfloat16 or wider, within the bound.
A program may use at most 128 MiB of HBM per device.

```python
import math
import jax
import jax.numpy as jnp
import numpy as np
from jax import lax

D = 8192
FF = 28672
QH = 64
KVH = 8
HD = 128
MID_LEN = 1024
LEAF = 256
ROOT = 16384
CAP = 8
BRANCHES = 32
MIDS = 8


def draw_queries(key, part):
    values = jnp.clip(jax.random.normal(jax.random.fold_in(key, 5), (BRANCHES, QH, HD), jnp.float32), -6.0, 6.0)
    return values.astype(jnp.bfloat16)


def draw_root_keys(key, part):
    values = jnp.clip(jax.random.normal(jax.random.fold_in(key, 9), (ROOT, KVH, HD), jnp.float32), -6.0, 6.0)
    return values.astype(jnp.bfloat16)


def touch_ends(values, own_key, smallest, largest):
    dims = values.shape
    place = [jax.random.randint(jax.random.fold_in(own_key, axis), (), 0, dims[axis]) for axis in range(len(dims))]
    values = values.at[tuple(place)].set(smallest)
    longest = dims.index(max(dims))
    place[longest] = (place[longest] + 1) % dims[longest]
    return values.at[tuple(place)].set(largest)


def block_scale(key, shape, split, low, largest):
    factor_of, own = 1.0, jax.random.fold_in(key, 6)
    for position, shards_of in split:
        draws = jnp.exp(jax.random.uniform(jax.random.fold_in(own, position), (shards_of,), jnp.float32, low / len(split), largest / len(split)))
        factor_of = factor_of * jnp.repeat(draws, shape[position] // shards_of).reshape([-1 if axis == position else 1 for axis in range(len(shape))])
    return factor_of


def assign_block(own_key, own, number, rows, number_of, top, limit, lean):
    ranking = jax.random.permutation(own_key, number_of)
    crowded, common = load_shares(number_of, rows * top, limit, lean, True), load_shares(number_of, rows * top, limit, lean, False)
    places = jnp.arange(number_of)

    def named(sizes, offset_by):
        used = int((sizes > 0).sum())
        fixed = max(1, used // 4)
        moved = fixed + (places - fixed + offset_by * (used - fixed)) % max(1, number_of - fixed)
        return jnp.zeros((number_of,), jnp.int32).at[ranking[jnp.where(places < fixed, places, moved)]].set(jnp.asarray(sizes, jnp.int32))

    sizes = jnp.where(number % 4 == 0, named(crowded, number // 4), named(common, number - number // 4 - 1))
    mixed = jax.random.permutation(jax.random.fold_in(own, 3), number_of)
    source_of, taker = mixed[0:number_of // 2 * 2:2], mixed[1:number_of // 2 * 2:2]
    slack = jnp.minimum(sizes[source_of] - 1, limit - sizes[taker]) // 2
    slack = jnp.where((source_of == ranking[0]) | (taker == ranking[0]) | (sizes[taker] == 0), 0, jnp.maximum(slack, 0))
    moved = jax.random.randint(jax.random.fold_in(own, 4), (number_of // 2,), 0, 1 << 20) % (slack + 1)
    sizes = sizes.at[source_of].add(-moved).at[taker].add(moved)
    labels = jnp.searchsorted(jnp.cumsum(sizes), jnp.arange(rows * top), side="right").astype(jnp.int32)
    grid = labels.reshape(top, rows).T
    grid = grid[jax.random.permutation(jax.random.fold_in(own, 1), rows)]
    offset_by = jax.random.randint(jax.random.fold_in(own, 2), (rows, 1), 0, top)
    return jnp.take_along_axis(grid, (jnp.arange(top)[None, :] + offset_by) % top, axis=1)


def load_shares(amount, total, limit, skew, full):
    portions = [(1 << 20) // math.isqrt(standing ** skew) + 1 for standing in range(1, amount + 1)]
    largest = limit if full else min(limit, max(-(-total // amount), total * portions[0] // sum(portions)))
    least = 1 if total - largest >= amount - 1 else 0
    counts, rest = [largest] + [least] * (amount - 1), total - largest - least * (amount - 1)
    while rest > 0:
        movable = [i for i in range(1, amount) if counts[i] < largest] or [i for i in range(1, amount) if counts[i] < limit]
        mass, budget = sum([portions[i] for i in movable]), rest
        for i in movable:
            addition = min(limit - counts[i], max(1, budget * portions[i] // mass), rest)
            counts[i] = counts[i] + addition
            rest = rest - addition
    return np.array(counts)


def scatter_about(key, dims, deviation, most, pieces=(), held_as=jnp.bfloat16):
    drawn = deviation * jax.random.normal(key, dims, jnp.float32)
    if pieces:
        drawn = drawn * block_scale(key, dims, pieces, -0.22, 0.18)
    return jnp.clip(drawn, -most, most).astype(held_as)


def setup_inputs(seed: int = 0) -> dict:
    key_of = jax.random.split(jax.random.key(seed), 17)
    queries = draw_queries(jax.random.fold_in(key_of[16], 71), 0)
    root_keys = draw_root_keys(jax.random.fold_in(key_of[16], 71), 0)
    root_values = scatter_about(key_of[2], (ROOT, KVH, HD), 1.0, 6.0, ((0, 8), (1, 4)))
    mid_keys = scatter_about(key_of[3], (MIDS, MID_LEN, KVH, HD), 1.0, 6.0, ((0, 8), (2, 4)))
    mid_values = scatter_about(key_of[4], (MIDS, MID_LEN, KVH, HD), 1.0, 6.0, ((0, 8), (2, 4)))
    leaf_keys = scatter_about(key_of[5], (BRANCHES, LEAF, KVH, HD), 1.0, 6.0, ((0, 8), (2, 4)))
    leaf_values = scatter_about(key_of[6], (BRANCHES, LEAF, KVH, HD), 1.0, 6.0, ((0, 8), (2, 4)))
    mid_length = touch_ends(jax.random.randint(key_of[7], (MIDS,), 1, MID_LEN + 1), jax.random.fold_in(key_of[7], 1), 1, MID_LEN).astype(jnp.int32)
    leaf_length = touch_ends(jax.random.randint(key_of[8], (BRANCHES,), 1, LEAF + 1), jax.random.fold_in(key_of[8], 1), 1, LEAF).astype(jnp.int32)
    branch_mid_keys = jax.random.split(jax.random.fold_in(key_of[9], 1), BRANCHES // BRANCHES)
    branch_mid_turns = jax.random.permutation(jax.random.fold_in(key_of[9], 3), BRANCHES // BRANCHES)
    branch_mid = jax.vmap(lambda own, number: assign_block(jax.random.fold_in(key_of[9], 2), own, number, BRANCHES, MIDS, 1, CAP, 2))(branch_mid_keys, branch_mid_turns).reshape((BRANCHES, 1))
    residual = scatter_about(key_of[10], (BRANCHES, D), 1.0, 6.0, ((1, 8),))
    norm_gain = jnp.clip(1.0 + 0.1 * jax.random.normal(key_of[11], (D,), jnp.float32), 0.5, 1.5)
    out_weight = scatter_about(key_of[12], (QH * HD, D), (QH * HD) ** -0.5, 0.0625, ((0, 4), (1, 8)))
    gate_weight = scatter_about(key_of[13], (D, FF), D ** -0.5, 0.0625, ((0, 8), (1, 4)))
    up_weight = scatter_about(key_of[14], (D, FF), D ** -0.5, 0.0625, ((0, 8), (1, 4)))
    down_weight = scatter_about(key_of[15], (FF, D), FF ** -0.5, 0.03125, ((0, 4), (1, 8)))
    return dict(queries=queries, root_keys=root_keys, root_values=root_values, mid_keys=mid_keys, mid_values=mid_values, leaf_keys=leaf_keys, leaf_values=leaf_values, mid_length=mid_length, leaf_length=leaf_length, branch_mid=branch_mid, residual=residual, norm_gain=norm_gain, out_weight=out_weight, gate_weight=gate_weight, up_weight=up_weight, down_weight=down_weight)


masked_score = -1e+30
norm_eps = 1e-05

def reference(queries, root_keys, root_values, mid_keys, mid_values, leaf_keys, leaf_values, mid_length, leaf_length, branch_mid, residual, norm_gain, out_weight, gate_weight, up_weight, down_weight):
    group_size = QH // KVH
    scaling = 1.0 / math.sqrt(HD)

    def attend(inputs):
        query_rows, mid_index, leaf_key, leaf_value, leaf_count = inputs
        key_block = jnp.concatenate([root_keys, mid_keys[mid_index], leaf_key], axis=0).astype(jnp.float32)
        value_block = jnp.concatenate([root_values, mid_values[mid_index], leaf_value], axis=0).astype(jnp.float32)
        mid_count = mid_length[mid_index]
        usable = jnp.concatenate([jnp.ones((ROOT,), dtype=bool), jnp.arange(MID_LEN) < mid_count, jnp.arange(LEAF) < leaf_count])
        grouped = query_rows.astype(jnp.float32).reshape(KVH, group_size, HD)
        scores = jnp.einsum('kgd,lkd->kgl', grouped, key_block, precision=lax.Precision.HIGHEST) * scaling
        scores = jnp.where(usable, scores, masked_score)
        highest = lax.optimization_barrier(jnp.max(scores, axis=-1, keepdims=True))
        weights = jnp.where(usable, jnp.exp(scores - highest), 0.0)
        rounded = weights.astype(jnp.bfloat16).astype(jnp.float32)
        weighted = jnp.einsum('kgl,lkd->kgd', rounded, value_block, precision=lax.Precision.HIGHEST)
        return (weighted / lax.optimization_barrier(jnp.sum(weights, axis=-1))[..., None]).reshape(QH * HD)
    attended = lax.map(attend, (queries, branch_mid[:, 0], leaf_keys, leaf_values, leaf_length)).astype(jnp.bfloat16)
    stream = residual.astype(jnp.float32) + jnp.dot(attended, out_weight, preferred_element_type=jnp.float32)
    mean_square = lax.optimization_barrier(jnp.sum(stream * stream, axis=1, keepdims=True)) / D
    normed = (stream * lax.rsqrt(mean_square + norm_eps) * norm_gain[None, :]).astype(jnp.bfloat16)
    gate = jnp.dot(normed, gate_weight, preferred_element_type=jnp.float32)
    upward = jnp.dot(normed, up_weight, preferred_element_type=jnp.float32)
    act = (jax.nn.silu(gate) * upward).astype(jnp.bfloat16)
    return (stream + jnp.dot(act, down_weight, preferred_element_type=jnp.float32)).astype(jnp.bfloat16)
```

```python
import functools
import math
from contextlib import nullcontext as scope

import jax
import jax.numpy as jnp
import numpy as np
from jax import lax
from jax.experimental import pallas as pl
from jax.experimental.pallas import tpu as pltpu
from jax.sharding import PartitionSpec as P

norm_eps = 1e-05
masked_score = -1e30
MESH = pl.DeviceIdType.MESH
ROWS = 128


def nt_dot(a, b):
    return lax.dot_general(a, b, (((1,), (1,)), ((), ())), preferred_element_type=jnp.float32)


def nn_dot(a, b):
    return jnp.dot(a, b, preferred_element_type=jnp.float32)


def to_lanes(columns):
    rows = columns[0].shape[0]
    lane = lax.broadcasted_iota(jnp.int32, (rows, 128), 1)
    grid = jnp.zeros((rows, 128), jnp.float32)
    for k, column in enumerate(columns):
        grid = jnp.where(lane == k, column, grid)
    if rows < 128:
        grid = jnp.concatenate([grid] * (128 // rows), axis=0)
    return grid.T


def layer_kernel(
    n, mp, owners, scale2, local_mids, mid_slots, leaf_slots, size, subs,
    mid_of, mid_len, leaf_len,
    q_hbm, order_hbm, res_hbm, gain_hbm,
    rk_hbm, rv_hbm, mk_hbm, mv_hbm, lk_hbm, lv_hbm, ow_hbm, gw_hbm, uw_hbm, dw_hbm,
    out_ref,
    q_raw, order_ref, res_ref, gain_ref, keys, values, ow, gw, uw, dw,
    q_own, qall, part_send, part_recv, st_send, st_recv, leaf_part, fac, att_own, att_all, lhs,
    pr_own, pr_hi, pr_pair, pr_lo, stream, sq_own, sq_all, xg,
    gx_send, gx_recv, own_sum, gz_send, gz_recv, act_all, acc, dn_send, dn_recv,
    in_sem, kv_sem, w_sem, q_s, q_r, p_s, p_r, t_s, t_r, a_s, a_r, s_s, s_r,
    h_s, h_r, l_s, l_r, gx_s, gx_r, gz_s, gz_r, cz_s, cz_r, cx_s, cx_r, d_s, d_r,
):
    me = lax.axis_index("node")
    mpi = lax.axis_index("mp")
    owned, local_heads, hd = q_raw.shape
    heads = local_heads // size
    own_rows = owned * size
    span = heads * hd
    chunk = act_all.shape[2]
    branches, width = stream.shape
    root = rk_hbm.shape[0]
    mids = mk_hbm.shape[0]
    shared = root + mids
    lo, hi = lax.rem(me, 2), me // 2
    partner = me + 1 - 2 * lo
    halves = n // 2
    owner_halves = owners // 2
    mp_lo, mp_hi = lax.rem(mpi, 2), mpi // 2
    mp_partner = mpi + 1 - 2 * mp_lo
    mp_halves = mp // 2

    in_copies = [
        pltpu.make_async_copy(src, dst, in_sem.at[k])
        for k, (src, dst) in enumerate(
            ((q_hbm, q_raw), (order_hbm, order_ref), (res_hbm, res_ref), (gain_hbm, gain_ref))
        )
    ]
    in_copies[0].start()
    kv_copies = []
    for side, (dst, parts) in enumerate(
        ((keys, (rk_hbm, mk_hbm, lk_hbm)), (values, (rv_hbm, mv_hbm, lv_hbm)))
    ):
        start = 0
        for k, src in enumerate(parts):
            rows = src.shape[0]
            copy = pltpu.make_async_copy(
                src, dst.at[pl.ds(start, rows), pl.ds(0, hd)], kv_sem.at[side * 3 + k]
            )
            copy.start()
            kv_copies.append(copy)
            start += rows
    for copy in in_copies[1:]:
        copy.start()
    w_copies = [
        pltpu.make_async_copy(src, dst, w_sem.at[k])
        for k, (src, dst) in enumerate(((ow_hbm, ow), (gw_hbm, gw), (uw_hbm, uw), (dw_hbm, dw)))
    ]

    barrier = pltpu.get_barrier_semaphore()

    def greet(axis, here, count):
        def body(i, carry):
            pl.semaphore_signal(
                barrier, inc=1, device_id={axis: lax.rem(here + i, count)}, device_id_type=MESH
            )
            return carry

        lax.fori_loop(1, count, body, 0)

    greet("node", me, n)
    greet("mp", mpi, mp)

    def remote(src, dst, send, recv, axis, peer):
        return pltpu.make_async_remote_copy(
            src_ref=src, dst_ref=dst, send_sem=send, recv_sem=recv,
            device_id={axis: peer}, device_id_type=MESH,
        )

    def peers(axis, fn):
        here, count = (me, n) if axis == "node" else (mpi, mp)

        def body(i, carry):
            fn(lax.rem(here + i, count))
            return carry

        lax.fori_loop(1, count, body, 0)

    def send_all(axis, src, dst, send, recv):
        here = me if axis == "node" else mpi
        peers(
            axis,
            lambda j: remote(src(j), dst.at[here], send.at[j], recv.at[here], axis, j).start(),
        )

    def wait_sends(axis, src, dst, send, recv):
        peers(axis, lambda j: remote(src(j), dst.at[j], send.at[j], recv.at[j], axis, j).wait_send())

    def wait_recvs(axis, src, dst, send, recv):
        peers(axis, lambda j: remote(src(j), dst.at[j], send.at[j], recv.at[j], axis, j).wait_recv())

    with scope("qprep"):
        in_copies[0].wait()
        raw_q = q_raw[...].astype(jnp.float32)
        for h in range(heads):
            q_own[:, h * hd:(h + 1) * hd] = (
                raw_q[:, h * size:(h + 1) * size, :].reshape(own_rows, hd).astype(jnp.bfloat16)
            )
        qall[me] = q_own[...]

    with scope("barrier"):
        pl.semaphore_wait(barrier, n - 1 + mp - 1)
    send_all("node", lambda j: q_own, qall, q_s, q_r)

    with scope("kvwait"):
        for copy in kv_copies:
            copy.wait()
    for copy in w_copies:
        copy.start()

    block = 256
    row = lax.broadcasted_iota(jnp.int32, (block, hd), 0)
    keep = [(lax.rem(row, heads) == h).astype(jnp.float32).astype(jnp.bfloat16) for h in range(heads)]

    def spread(i, carry):
        at = pl.ds(pl.multiple_of(i * block, block), block)
        for ref in (keys, values):
            mixed = ref[at, 0:hd]
            for h in range(heads):
                ref[at, h * hd:(h + 1) * hd] = mixed * keep[h]
        return carry

    with scope("spread"):
        lax.fori_loop(0, keys.shape[0] // block, spread, 0)

    def softmax_parts(pieces, rows):
        lane = lax.broadcasted_iota(jnp.int32, (rows, 128), 1)
        top = None
        for piece in pieces:
            for k in range(piece.shape[1] // 128):
                part = piece[:, k * 128:(k + 1) * 128]
                top = part if top is None else jnp.maximum(top, part)
        tops, mixed_top = [], None
        for h in range(heads):
            mine = lax.rem(lane, heads) == h
            peak = jnp.max(jnp.where(mine, top, -jnp.inf), axis=1, keepdims=True)
            tops.append(peak)
            mixed_top = jnp.broadcast_to(peak, lane.shape) if h == 0 else jnp.where(mine, peak, mixed_top)
        weights, total = [], None
        for piece in pieces:
            parts = []
            for k in range(piece.shape[1] // 128):
                part = jnp.exp2((piece[:, k * 128:(k + 1) * 128] - mixed_top) * scale2)
                total = part if total is None else total + part
                parts.append(part.astype(jnp.bfloat16))
            weights.append(jnp.concatenate(parts, axis=1))
        totals = [
            jnp.sum(jnp.where(lax.rem(lane, heads) == h, total, 0.0), axis=1, keepdims=True)
            for h in range(heads)
        ]
        return tops, totals, weights

    with scope("leaf"):
        leaf_rows = leaf_slots * heads
        stats = []
        for b in range(owned):
            at = pl.ds(shared + b * leaf_rows, leaf_rows)
            scores = nt_dot(q_own[b * size:(b + 1) * size, :], keys[at, :])
            column = lax.broadcasted_iota(jnp.int32, scores.shape, 1)
            scores = jnp.where(column < leaf_len[b] * heads, scores, masked_score)
            tops, totals, weights = softmax_parts([scores], size)
            leaf_part[b * size:(b + 1) * size, :] = nn_dot(weights[0], values[at, :])
            stats.append(tops + totals)
        leaf_stats = to_lanes([
            jnp.concatenate([stats[b][k] for b in range(owned)], axis=0) for k in range(2 * heads)
        ])[0:8]

    group = max(1, min(n, ROWS // own_rows))
    rows = group * own_rows
    group_branches = group * owned
    groups = n // group

    def attend(i, carry):
        g = lax.rem(me // group + i, groups)

        def each(fn):
            for k in range(group):
                j = g * group + k
                pl.when(j != me)(functools.partial(fn, j))

        each(lambda j: remote(q_own, qall.at[j], q_s.at[j], q_r.at[j], "node", j).wait_recv())
        lows, highs = [], []
        for b in range(group_branches):
            mid = mid_of[g * group_branches + b]
            local = mid - me * local_mids
            here = (local >= 0) & (local < local_mids)
            low = local * (mid_slots * heads)
            highs.append(jnp.full((size, 128), jnp.where(here, low + mid_len[mid] * heads, 0), jnp.int32))
            lows.append(jnp.full((size, 128), jnp.where(here, low, 0), jnp.int32))
        low, high = jnp.concatenate(lows, axis=0), jnp.concatenate(highs, axis=0)
        query = qall[pl.ds(g * group, group)].reshape(rows, span)
        root_scores = nt_dot(query, keys[0:root, :])
        mid_scores = nt_dot(query, keys[root:shared, :])
        lane = lax.broadcasted_iota(jnp.int32, (rows, 128), 1)
        seen_scores = []
        for k in range(mids // 128):
            column = lane + k * 128
            seen = column < high
            if local_mids > 1:
                seen = seen & (column >= low)
            seen_scores.append(jnp.where(seen, mid_scores[:, k * 128:(k + 1) * 128], masked_score))
        tops, totals, weights = softmax_parts([root_scores] + seen_scores, rows)
        weighted = nn_dot(weights[0], values[0:root, :]) + nn_dot(
            jnp.concatenate(weights[1:], axis=1), values[root:shared, :]
        )
        part_send[pl.ds(g * group, group)] = weighted.astype(jnp.bfloat16).reshape(group, own_rows, span)
        st_send[g] = to_lanes(tops + totals)[0:8]

        def send(j):
            remote(part_send.at[j], part_recv.at[me], p_s.at[j], p_r.at[me], "node", j).start()
            remote(st_send.at[g], st_recv.at[me], t_s.at[j], t_r.at[me], "node", j).start()

        each(send)
        return carry

    with scope("attend"):
        lax.fori_loop(0, groups, attend, 0)
    part_recv[me] = part_send[me]
    st_recv[me] = st_send[me // group]
    with scope("partx"):
        wait_recvs("node", lambda j: part_send.at[j], part_recv, p_s, p_r)
        wait_recvs("node", lambda j: st_send.at[0], st_recv, t_s, t_r)

    with scope("merge"):
        blocks = []
        leaf_factors = []
        for h in range(heads):
            peak = jnp.concatenate([st_recv[i, h:h + 1, :] for i in range(n)], axis=0)
            total = jnp.concatenate([st_recv[i, heads + h:heads + h + 1, :] for i in range(n)], axis=0)
            leaf_peak, leaf_total = leaf_stats[h:h + 1], leaf_stats[heads + h:heads + h + 1]
            top = jnp.maximum(jnp.max(peak, axis=0, keepdims=True), leaf_peak)
            scale, leaf_scale = jnp.exp2((peak - top) * scale2), jnp.exp2((leaf_peak - top) * scale2)
            whole = jnp.sum(total * scale, axis=0, keepdims=True) + leaf_total * leaf_scale
            blocks.append(scale / whole)
            leaf_factors.append(leaf_scale / whole)
        used = heads * n + heads
        table = jnp.concatenate(
            blocks + leaf_factors + [jnp.zeros((128 - used, 128), jnp.float32)], axis=0
        )
        fac[...] = table.T
        mine = fac[pl.ds(pl.multiple_of(lax.rem(me, group) * own_rows, own_rows), own_rows), :]
        for h in range(heads):
            at = slice(h * hd, (h + 1) * hd)
            sum_h = leaf_part[:, at] * mine[:, heads * n + h:heads * n + h + 1]
            for i in range(n):
                sum_h = sum_h + part_recv[i, :, at].astype(jnp.float32) * mine[:, h * n + i:h * n + i + 1]
            att_own[:, at] = sum_h.astype(jnp.bfloat16)

    with scope("attag"):
        send_all("node", lambda j: att_own, att_all, a_s, a_r)
        att_all[me] = att_own[...]
        in_copies[1].wait()
        wait_recvs("node", lambda j: att_own, att_all, a_s, a_r)

    with scope("order"):
        mixed = nn_dot(order_ref[...], att_all[...].reshape(n * own_rows, span)).astype(jnp.bfloat16)
        for h in range(heads):
            for g in range(size):
                first = (h * size + g) * hd
                lhs[:, first:first + hd] = mixed[g * branches:(g + 1) * branches, h * hd:(h + 1) * hd]

    w_copies[0].wait()
    tiles, tile = pr_own.shape[0], pr_own.shape[2]

    def mp_peer(k):
        return lax.rem(mp_hi + k, mp_halves) * 2 + mp_lo

    def project(t, carry):
        at = pl.ds(pl.multiple_of(t * tile, tile), tile)
        value = nn_dot(lhs[...], ow[:, at])
        stream[:, at] = value
        pr_own[t] = value.astype(jnp.bfloat16)
        for k in range(1, mp_halves):
            peer = mp_peer(k)
            remote(
                pr_own.at[t], pr_hi.at[mp_hi, t], h_s.at[peer // 2, t], h_r.at[mp_hi, t], "mp", peer
            ).start()
        return carry

    def pair(t, carry):
        at = pl.ds(pl.multiple_of(t * tile, tile), tile)
        value = stream[:, at]
        for k in range(1, mp_halves):
            peer = mp_peer(k)
            at_hi = peer // 2
            remote(
                pr_own.at[t], pr_hi.at[at_hi, t], h_s.at[at_hi, t], h_r.at[at_hi, t], "mp", peer
            ).wait()
            value = value + pr_hi[at_hi, t].astype(jnp.float32)
        stream[:, at] = value
        pr_pair[t] = value.astype(jnp.bfloat16)
        remote(pr_pair.at[t], pr_lo.at[t], l_s.at[t], l_r.at[t], "mp", mp_partner).start()
        return carry

    def finish(t, squares):
        at = pl.ds(pl.multiple_of(t * tile, tile), tile)
        remote(pr_pair.at[t], pr_lo.at[t], l_s.at[t], l_r.at[t], "mp", mp_partner).wait()
        value = stream[:, at] + pr_lo[t].astype(jnp.float32) + res_ref[:, at].astype(jnp.float32)
        stream[:, at] = value
        xg[:, at] = (value * gain_ref[:, at]).astype(jnp.bfloat16)
        return squares + jnp.sum(value * value, axis=1, keepdims=True)

    with scope("project"):
        lax.fori_loop(0, tiles, project, 0)
    with scope("prhi"):
        in_copies[2].wait()
        in_copies[3].wait()
        lax.fori_loop(0, tiles, pair, 0)
    with scope("prlo"):
        squares = lax.fori_loop(0, tiles, finish, jnp.zeros((branches, 1), jnp.float32))
        sq_own[...] = to_lanes([squares])[0:8]
        send_all("node", lambda j: sq_own, sq_all, s_s, s_r)
        sq_all[me] = sq_own[...]

    with scope("wwait12"):
        w_copies[1].wait()
        w_copies[2].wait()

    def turn(i):
        down = jnp.where(owner_halves - 1 - i > hi, owner_halves - 1 - i, owner_halves - 2 - i)
        up = jnp.where(i < hi, i, i + 1)
        other = jnp.where(2 * hi >= owner_halves, up, down)
        return jnp.where((i == owner_halves - 1) & (hi < owner_halves), hi, other)

    def gate_up(j, off, count):
        at = pl.ds(pl.multiple_of(j * chunk + off, 128), count)
        return nn_dot(xg[...], gw[:, at]), nn_dot(xg[...], uw[:, at])

    def gx(k, s):
        at = pl.ds(subs[s][0], subs[s][1])
        return remote(
            gx_send.at[k, :, :, at], gx_recv.at[k, :, :, at], gx_s.at[k, s], gx_r.at[k, s], "node", partner
        )

    def gz(k, slot, s, recv_at):
        at = pl.ds(subs[s][0], subs[s][1])
        return remote(
            gz_send.at[k, :, :, at], gz_recv.at[slot, :, :, at], gz_s.at[k, s], gz_r.at[recv_at, s],
            "node", k * 2 + lo,
        )

    def partner_side(i, carry):
        k = turn(i)
        for s, (off, count) in enumerate(subs):
            gate, upward = gate_up(k * 2 + 1 - lo, off, count)
            gx_send[k, 0, :, off:off + count] = gate.astype(jnp.bfloat16)
            gx_send[k, 1, :, off:off + count] = upward.astype(jnp.bfloat16)
            gx(k, s).start()
        return carry

    def own_side(i, carry):
        k = turn(i)
        for s, (off, count) in enumerate(subs):
            at = slice(off, off + count)
            gate, upward = gate_up(k * 2 + lo, off, count)
            gx(k, s).wait_recv()
            gate = gate + gx_recv[k, 0, :, at].astype(jnp.float32)
            upward = upward + gx_recv[k, 1, :, at].astype(jnp.float32)

            @pl.when(k == hi)
            def _():
                own_sum[0, :, at] = gate
                own_sum[1, :, at] = upward

            @pl.when(k != hi)
            def _():
                gz_send[k, 0, :, at] = gate.astype(jnp.bfloat16)
                gz_send[k, 1, :, at] = upward.astype(jnp.bfloat16)
                gz(k, hi, s, hi).start()

        return carry

    with scope("gupartner"):
        lax.fori_loop(0, owner_halves, partner_side, 0)
    with scope("guown"):
        lax.fori_loop(0, owner_halves, own_side, 0)
    with scope("sqwait"):
        wait_recvs("node", lambda j: sq_own, sq_all, s_s, s_r)

    def act_z(k, owner, sem_at):
        return remote(
            act_all.at[owner], act_all.at[owner], cz_s.at[k], cz_r.at[sem_at], "node", k * 2 + lo
        )

    def act_x(k, side):
        owner = k * 2 + side
        return remote(act_all.at[owner], act_all.at[owner], cx_s.at[k], cx_r.at[k], "node", partner)

    def other_halves(fn):
        def body(i, carry):
            far = jnp.where(2 * hi >= halves, jnp.where(i < hi, i, i + 1),
                            jnp.where(halves - 1 - i > hi, halves - 1 - i, halves - 2 - i))
            fn(far)
            return carry

        lax.fori_loop(0, halves - 1, body, 0)

    def owner_work():
        total = sq_all[0]
        for k in range(1, n):
            total = total + sq_all[k]
        column = jnp.concatenate([total] * 16, axis=0).T[0:branches, 0:1]
        root_mean = lax.rsqrt(column / (width * n) + norm_eps)
        for s, (off, count) in enumerate(subs):
            at = slice(off, off + count)
            other_halves(lambda k: gz(0, k, s, k).wait_recv())

            def add(i, carry):
                k = lax.rem(hi + i, halves)
                return (
                    carry[0] + gz_recv[k, 0, :, at].astype(jnp.float32),
                    carry[1] + gz_recv[k, 1, :, at].astype(jnp.float32),
                )

            gate, upward = lax.fori_loop(1, halves, add, (own_sum[0, :, at], own_sum[1, :, at]))
            gate, upward = gate * root_mean, upward * root_mean
            act_all[me, :, at] = (gate / (1.0 + jnp.exp(-gate)) * upward).astype(jnp.bfloat16)
        act_x(hi, lo).start()
        other_halves(lambda k: act_z(k, me, hi).start())

    with scope("ownerwork"):
        if owners == n:
            owner_work()
        else:
            pl.when(me < owners)(owner_work)

    w_copies[3].wait()
    acc[...] = jnp.zeros(acc.shape, jnp.float32)

    def down(owner):
        at = pl.ds(pl.multiple_of(owner * chunk, 128), chunk)
        acc[...] += nn_dot(act_all[owner], dw[at, :])

    def down_own(i, carry):
        k = turn(owner_halves - 1 - i)

        @pl.when(k != hi)
        def _():
            act_z(k, k * 2 + lo, k).wait_recv()
            act_x(k, lo).start()

        down(k * 2 + lo)
        return carry

    def down_partner(i, carry):
        k = turn(owner_halves - 1 - i)
        act_x(k, 1 - lo).wait_recv()
        down(k * 2 + 1 - lo)
        return carry

    with scope("down1"):
        lax.fori_loop(0, owner_halves, down_own, 0)
    with scope("down2"):
        lax.fori_loop(0, owner_halves, down_partner, 0)

    rows_out = out_ref.shape[0]
    with scope("dnx"):
        for k in range(mp):
            dn_send[k] = acc[k * rows_out:(k + 1) * rows_out, :].astype(jnp.bfloat16)
        send_all("mp", lambda j: dn_send.at[j], dn_recv, d_s, d_r)
        dn_recv[mpi] = dn_send[mpi]
        wait_recvs("mp", lambda j: dn_send.at[j], dn_recv, d_s, d_r)
        total = dn_recv[0].astype(jnp.float32)
        for k in range(1, mp):
            total = total + dn_recv[k].astype(jnp.float32)
        own = stream[pl.ds(pl.multiple_of(mpi * rows_out, rows_out), rows_out), :]
        out_ref[...] = (own + total).astype(jnp.bfloat16)

    with scope("drain"):
        wait_sends("node", lambda j: q_own, qall, q_s, q_r)
        wait_sends("node", lambda j: part_send.at[j], part_recv, p_s, p_r)
        wait_sends("node", lambda j: st_send.at[0], st_recv, t_s, t_r)
        wait_sends("node", lambda j: att_own, att_all, a_s, a_r)
        wait_sends("node", lambda j: sq_own, sq_all, s_s, s_r)
        wait_sends("mp", lambda j: dn_send.at[j], dn_recv, d_s, d_r)

        def sent(k, carry):
            for s in range(len(subs)):
                gx(k, s).wait_send()
                pl.when(k != hi)(lambda s=s: gz(k, hi, s, hi).wait_send())
            act_x(k, lo).wait_send()
            return carry

        lax.fori_loop(0, owner_halves, sent, 0)

        def acts_sent():
            other_halves(lambda k: act_z(k, me, hi).wait_send())

        if owners == n:
            acts_sent()
        else:
            pl.when(me < owners)(acts_sent)


def on_device(
    n, mp,
    queries, root_keys, root_values, mid_keys, mid_values, leaf_keys, leaf_values,
    mid_length, leaf_length, branch_mid, residual, norm_gain,
    out_weight, gate_weight, up_weight, down_weight,
):
    owned, local_heads, hd = queries.shape
    heads = root_keys.shape[1]
    size = local_heads // heads
    own_rows = owned * size
    branches = owned * n
    width = residual.shape[1]
    hidden = gate_weight.shape[1]
    lane_tiles = hidden // 128
    owners = max(k for k in range(2, n + 1, 2) if lane_tiles % k == 0)
    chunk = hidden // owners
    first = (chunk // 128 + 1) // 2 * 128
    subs = ((0, first), (first, chunk - first)) if first < chunk else ((0, chunk),)
    mid_slots = mid_keys.shape[1]
    leaf_slots = leaf_keys.shape[1]
    local_mids = mid_keys.shape[0]
    halves, owner_halves, mp_halves = n // 2, owners // 2, mp // 2
    group = max(1, min(n, ROWS // own_rows))
    tile = math.gcd(width, 256)
    tiles = width // tile

    order = np.zeros((branches * size, branches * size), np.float32)
    at = np.arange(branches * size)
    order[(at % size) * branches + at // size, at] = 1.0

    flat = [
        a.reshape(-1, hd)
        for a in (root_keys, root_values, mid_keys, mid_values, leaf_keys, leaf_values)
    ]
    kv_rows = flat[0].shape[0] + flat[2].shape[0] + flat[4].shape[0]
    span = heads * hd
    bf, f32 = jnp.bfloat16, jnp.float32
    dma = pltpu.SemaphoreType.DMA
    vmem = pl.BlockSpec(memory_space=pltpu.VMEM)
    smem = pl.BlockSpec(memory_space=pltpu.SMEM)
    hbm = pl.BlockSpec(memory_space=pl.ANY)
    rows_out = branches // mp
    scratch = [
        pltpu.VMEM((owned, local_heads, hd), bf),
        pltpu.VMEM(order.shape, bf),
        pltpu.VMEM((branches, width), bf),
        pltpu.VMEM((1, width), f32),
        pltpu.VMEM((kv_rows, span), bf),
        pltpu.VMEM((kv_rows, span), bf),
        pltpu.VMEM(out_weight.shape, bf),
        pltpu.VMEM(gate_weight.shape, bf),
        pltpu.VMEM(up_weight.shape, bf),
        pltpu.VMEM(down_weight.shape, bf),
        pltpu.VMEM((own_rows, span), bf),
        pltpu.VMEM((n, own_rows, span), bf),
        pltpu.VMEM((n, own_rows, span), bf),
        pltpu.VMEM((n, own_rows, span), bf),
        pltpu.VMEM((n // group, 8, 128), f32),
        pltpu.VMEM((n, 8, 128), f32),
        pltpu.VMEM((own_rows, span), f32),
        pltpu.VMEM((128, 128), f32),
        pltpu.VMEM((own_rows, span), bf),
        pltpu.VMEM((n, own_rows, span), bf),
        pltpu.VMEM((branches, local_heads * hd), bf),
        pltpu.VMEM((tiles, branches, tile), bf),
        pltpu.VMEM((mp_halves, tiles, branches, tile), bf),
        pltpu.VMEM((tiles, branches, tile), bf),
        pltpu.VMEM((tiles, branches, tile), bf),
        pltpu.VMEM((branches, width), f32),
        pltpu.VMEM((8, 128), f32),
        pltpu.VMEM((n, 8, 128), f32),
        pltpu.VMEM((branches, width), bf),
        pltpu.VMEM((owner_halves, 2, branches, chunk), bf),
        pltpu.VMEM((owner_halves, 2, branches, chunk), bf),
        pltpu.VMEM((2, branches, chunk), f32),
        pltpu.VMEM((owner_halves, 2, branches, chunk), bf),
        pltpu.VMEM((halves, 2, branches, chunk), bf),
        pltpu.VMEM((owners, branches, chunk), bf),
        pltpu.VMEM((branches, width), f32),
        pltpu.VMEM((mp, rows_out, width), bf),
        pltpu.VMEM((mp, rows_out, width), bf),
        dma((4,)),
        dma((6,)),
        dma((4,)),
    ] + [dma((n,))] * 10 + [
        dma((mp_halves, tiles)),
        dma((mp_halves, tiles)),
        dma((tiles,)),
        dma((tiles,)),
        dma((owner_halves, len(subs))),
        dma((owner_halves, len(subs))),
        dma((owner_halves, len(subs))),
        dma((halves, len(subs))),
        dma((halves,)),
        dma((owner_halves,)),
        dma((owner_halves,)),
        dma((owner_halves,)),
        dma((mp,)),
        dma((mp,)),
    ]
    scale2 = hd ** -0.5 * math.log2(math.e)
    return pl.pallas_call(
        functools.partial(
            layer_kernel, n, mp, owners, scale2, local_mids, mid_slots, leaf_slots, size, subs
        ),
        out_shape=jax.ShapeDtypeStruct((rows_out, width), bf),
        in_specs=[smem] * 3 + [hbm] * 14,
        out_specs=vmem,
        scratch_shapes=scratch,
        compiler_params=pltpu.CompilerParams(
            collective_id=0, has_side_effects=True, vmem_limit_bytes=67043328
        ),
    )(
        branch_mid.reshape(-1), mid_length, leaf_length,
        queries, jnp.asarray(order, bf), residual, norm_gain[None, :],
        *flat, out_weight, gate_weight, up_weight, down_weight,
    )


def solution(mesh):
    in_specs = (
        P("node", "mp", None),
        P("node", "mp", None),
        P("node", "mp", None),
        P("node", None, "mp", None),
        P("node", None, "mp", None),
        P("node", None, "mp", None),
        P("node", None, "mp", None),
        P(),
        P("node"),
        P(),
        P(None, "node"),
        P("node"),
        P("mp", "node"),
        P("node", "mp"),
        P("node", "mp"),
        P("mp", "node"),
    )
    body = functools.partial(on_device, mesh.shape["node"], mesh.shape["mp"])
    return jax.shard_map(
        body, mesh=mesh, in_specs=in_specs, out_specs=P("mp", "node"), check_vma=False
    )
```

```python
import functools
import math
from contextlib import nullcontext as scope

import jax
import jax.numpy as jnp
import numpy as np
from jax import lax
from jax.experimental import pallas as pl
from jax.experimental.pallas import tpu as pltpu
from jax.sharding import PartitionSpec as P

norm_eps = 1e-05
masked_score = -1e30
MESH = pl.DeviceIdType.MESH
ROWS = 256


def nt_dot(a, b):
    return lax.dot_general(a, b, (((1,), (1,)), ((), ())), preferred_element_type=jnp.float32)


def nn_dot(a, b):
    return jnp.dot(a, b, preferred_element_type=jnp.float32)


def to_lanes(columns):
    rows = columns[0].shape[0]
    lane = lax.broadcasted_iota(jnp.int32, (rows, 128), 1)
    grid = jnp.zeros((rows, 128), jnp.float32)
    for k, column in enumerate(columns):
        grid = jnp.where(lane == k, column, grid)
    if rows < 128:
        grid = jnp.concatenate([grid] * (128 // rows), axis=0)
    return grid.T


def layer_kernel(
    n, mp, owners, scale2, local_mids, mid_slots, leaf_slots, size, subs,
    mid_of, mid_len, leaf_len,
    q_hbm, order_hbm, res_hbm, gain_hbm,
    rk_hbm, rv_hbm, mk_hbm, mv_hbm, lk_hbm, lv_hbm, ow_hbm, gw_hbm, uw_hbm, dw_hbm,
    out_ref,
    q_raw, order_ref, res_ref, gain_ref, keys, values, ow, gw, uw, dw,
    q_own, qall, part_send, part_recv, st_send, st_recv, leaf_part, fac, att_own, att_all, lhs,
    pr_own, pr_hi, pr_pair, pr_lo, stream, sq_own, sq_all, sq_own_scale, xg,
    gx_send, gx_recv, own_sum, gz_send, gz_recv, act_all, acc, dn_send, dn_recv,
    in_sem, kv_sem, w_sem, q_s, q_r, p_s, p_r, t_s, t_r, a_s, a_r, s_s, s_r,
    h_s, h_r, l_s, l_r, gx_s, gx_r, gz_s, gz_r, cz_s, cz_r, cx_s, cx_r, d_s, d_r,
):
    me = lax.axis_index("node")
    mpi = lax.axis_index("mp")
    owned, local_heads, hd = q_raw.shape
    heads = local_heads // size
    own_rows = owned * size
    span = heads * hd
    chunk = act_all.shape[2]
    branches, width = stream.shape
    root = rk_hbm.shape[0]
    mids = mk_hbm.shape[0]
    shared = root + mids
    lo, hi = lax.rem(me, 2), me // 2
    partner = me + 1 - 2 * lo
    halves = n // 2
    owner_halves = owners // 2
    mp_lo, mp_hi = lax.rem(mpi, 2), mpi // 2
    mp_partner = mpi + 1 - 2 * mp_lo
    mp_halves = mp // 2

    barrier = pltpu.get_barrier_semaphore()

    def greet(axis, here, count):
        def body(i, carry):
            pl.semaphore_signal(
                barrier, inc=1, device_id={axis: lax.rem(here + i, count)}, device_id_type=MESH
            )
            return carry

        lax.fori_loop(1, count, body, 0)

    greet("node", me, n)
    greet("mp", mpi, mp)

    in_copies = [
        pltpu.make_async_copy(src, dst, in_sem.at[k])
        for k, (src, dst) in enumerate(
            ((q_hbm, q_raw), (order_hbm, order_ref), (res_hbm, res_ref), (gain_hbm, gain_ref))
        )
    ]
    in_copies[0].start()
    for side, (dst, parts) in enumerate(
        ((keys, (rk_hbm, mk_hbm, lk_hbm)), (values, (rv_hbm, mv_hbm, lv_hbm)))
    ):
        start = 0
        for src in parts:
            rows = src.shape[0]
            pltpu.make_async_copy(
                src, dst.at[pl.ds(start, rows), pl.ds(0, hd)], kv_sem.at[side]
            ).start()
            start += rows
    for copy in in_copies[1:]:
        copy.start()
    w_copies = [
        pltpu.make_async_copy(src, dst, w_sem.at[k])
        for k, (src, dst) in enumerate(((ow_hbm, ow), (gw_hbm, gw), (uw_hbm, uw), (dw_hbm, dw)))
    ]

    def remote(src, dst, send, recv, axis, peer):
        return pltpu.make_async_remote_copy(
            src_ref=src, dst_ref=dst, send_sem=send, recv_sem=recv,
            device_id={axis: peer}, device_id_type=MESH,
        )

    def peers(axis, fn):
        here, count = (me, n) if axis == "node" else (mpi, mp)

        def body(i, carry):
            fn(lax.rem(here + i, count))
            return carry

        lax.fori_loop(1, count, body, 0)

    def send_all(axis, src, dst, send, recv):
        here = me if axis == "node" else mpi
        peers(axis, lambda j: remote(src(j), dst.at[here], send, recv, axis, j).start())

    def settle(ref, sem):
        pltpu.make_async_copy(ref, ref, sem).wait()

    def others(ref, count):
        return ref.at[pl.ds(0, count - 1)]

    with scope("qprep"):
        in_copies[0].wait()
        raw_q = q_raw[...].astype(jnp.float32)
        for h in range(heads):
            q_own[:, h * hd:(h + 1) * hd] = (
                raw_q[:, h * size:(h + 1) * size, :].reshape(own_rows, hd).astype(jnp.bfloat16)
            )
        qall[me] = q_own[...]

    with scope("barrier"):
        pl.semaphore_wait(barrier, n - 1 + mp - 1)
    group = max(1, min(n, ROWS // own_rows))
    groups = n // group

    def send_query(j):
        remote(q_own, qall.at[me], q_s, q_r.at[me // group], "node", j).start()

    def send_near(k, carry):
        send_query(me // group * group + lax.rem(me + k, group))
        return carry

    def send_far(k, carry):
        send_query(lax.rem(me // group * group + k, n))
        return carry

    lax.fori_loop(1, group, send_near, 0)
    lax.fori_loop(group, n, send_far, 0)

    with scope("kvwait"):
        for side, ref in enumerate((keys, values)):
            arrived = ref.at[:, pl.ds(0, hd)]
            pltpu.make_async_copy(arrived, arrived, kv_sem.at[side]).wait()
    for copy in w_copies:
        copy.start()

    block = math.gcd(512, math.gcd(shared, leaf_slots * heads))
    row = lax.broadcasted_iota(jnp.int32, (block, hd), 0)
    keep = [(lax.rem(row, heads) == h).astype(jnp.float32).astype(jnp.bfloat16) for h in range(heads)]

    def spread(i, carry):
        at = pl.ds(pl.multiple_of(i * block, block), block)
        for ref in (keys, values):
            mixed = ref[at, 0:hd]
            for h in range(heads):
                ref[at, h * hd:(h + 1) * hd] = mixed * keep[h]
        return carry

    with scope("spread"):
        lax.fori_loop(0, shared // block, spread, 0)

    def attend_rows(query, spans, seen):
        rows = query.shape[0]
        lane = lax.broadcasted_iota(jnp.int32, (rows, 128), 1)
        mine = [lax.rem(lane, heads) == h for h in range(heads)]

        def mix(columns):
            mixed = jnp.broadcast_to(columns[0], lane.shape)
            for h in range(1, heads):
                mixed = jnp.where(mine[h], columns[h], mixed)
            return mixed

        peaks, total, weighted = None, None, None
        for start, count in spans:
            scores = nt_dot(query, keys[start:start + count, :])
            parts = [
                seen(start + k, scores[:, k:k + 128], lane) for k in range(0, count, 128)
            ]
            top = functools.reduce(jnp.maximum, parts)
            now = [
                jnp.max(jnp.where(mine[h], top, -jnp.inf), axis=1, keepdims=True) for h in range(heads)
            ]
            if peaks is not None:
                now = [jnp.maximum(a, b) for a, b in zip(peaks, now)]
                shrink = [jnp.exp2((a - b) * scale2) for a, b in zip(peaks, now)]
                total = total * mix(shrink)
                weighted = weighted * jnp.concatenate(
                    [jnp.broadcast_to(a, (rows, hd)) for a in shrink], axis=1
                )
            peaks = now
            mixed = mix(peaks)
            rounded = []
            for part in parts:
                part = jnp.exp2((part - mixed) * scale2)
                total = part if total is None else total + part
                rounded.append(part.astype(jnp.bfloat16))
            product = nn_dot(jnp.concatenate(rounded, axis=1), values[start:start + count, :])
            weighted = product if weighted is None else weighted + product
        totals = [
            jnp.sum(jnp.where(mine[h], total, 0.0), axis=1, keepdims=True) for h in range(heads)
        ]
        return peaks, totals, weighted

    pack = min(group, 128 // own_rows)
    blocks = group // pack
    rows = group * own_rows
    group_branches = group * owned
    piece = math.gcd(2048, math.gcd(root, mids))

    def attend(i, carry):
        g = lax.rem(me // group + i, groups)

        def each(fn):
            for k in range(group):
                j = g * group + k
                pl.when(j != me)(functools.partial(fn, j))

        pl.when(g == me // group)(lambda: settle(qall.at[pl.ds(0, group - 1)], q_r.at[g]))
        if groups > 1:
            pl.when(g != me // group)(lambda: settle(qall.at[pl.ds(0, group)], q_r.at[g]))
        lows, highs = [], []
        for b in range(group_branches):
            mid = mid_of[g * group_branches + b]
            local = mid - me * local_mids
            here = (local >= 0) & (local < local_mids)
            low = local * (mid_slots * heads)
            highs.append(jnp.full((size, 128), jnp.where(here, low + mid_len[mid] * heads, 0), jnp.int32))
            lows.append(jnp.full((size, 128), jnp.where(here, low, 0), jnp.int32))
        low, high = jnp.concatenate(lows, axis=0), jnp.concatenate(highs, axis=0)
        query = qall[pl.ds(g * group, group)].reshape(rows, span)

        def seen(start, part, lane):
            if start < root:
                return part
            column = lane + (start - root)
            kept = column < high
            if local_mids > 1:
                kept = kept & (column >= low)
            return jnp.where(kept, part, masked_score)

        tops, totals, weighted = attend_rows(
            query, [(start, piece) for start in range(0, shared, piece)], seen
        )
        part_send[pl.ds(g * group, group)] = weighted.astype(jnp.bfloat16).reshape(group, own_rows, span)
        columns = tops + totals
        for k in range(blocks):
            at = slice(k * pack * own_rows, (k + 1) * pack * own_rows)
            st_send[g * blocks + k] = to_lanes([column[at] for column in columns])[0:8]

        def send(j):
            remote(part_send.at[j], part_recv.at[me], p_s, p_r, "node", j).start()
            remote(st_send.at[j // pack], st_recv.at[me], t_s, t_r, "node", j).start()

        each(send)
        return carry

    with scope("attend"):
        lax.fori_loop(0, groups, attend, 0)
    part_recv[me] = part_send[me]
    st_recv[me] = st_send[me // pack]

    with scope("leaf"):
        lax.fori_loop(shared // block, keys.shape[0] // block, spread, 0)
        leaf_rows = leaf_slots * heads
        stats = []
        for b in range(owned):
            start = shared + b * leaf_rows
            tops, totals, weighted = attend_rows(
                q_own[b * size:(b + 1) * size, :],
                [(start, leaf_rows)],
                lambda at, part, lane: jnp.where(
                    lane + (at - start) < leaf_len[b] * heads, part, masked_score
                ),
            )
            leaf_part[b * size:(b + 1) * size, :] = weighted
            stats.append(tops + totals)
        leaf_stats = to_lanes([
            jnp.concatenate([stats[b][k] for b in range(owned)], axis=0) for k in range(2 * heads)
        ])[0:8]

    with scope("partx"):
        settle(others(part_recv, n), p_r)
        settle(others(st_recv, n), t_r)

    with scope("merge"):
        factors = []
        leaf_factors = []
        for h in range(heads):
            peak = jnp.concatenate([st_recv[i, h:h + 1, :] for i in range(n)], axis=0)
            total = jnp.concatenate([st_recv[i, heads + h:heads + h + 1, :] for i in range(n)], axis=0)
            leaf_peak, leaf_total = leaf_stats[h:h + 1], leaf_stats[heads + h:heads + h + 1]
            top = jnp.maximum(jnp.max(peak, axis=0, keepdims=True), leaf_peak)
            scale, leaf_scale = jnp.exp2((peak - top) * scale2), jnp.exp2((leaf_peak - top) * scale2)
            whole = jnp.sum(total * scale, axis=0, keepdims=True) + leaf_total * leaf_scale
            factors.append(scale / whole)
            leaf_factors.append(leaf_scale / whole)
        used = heads * n + heads
        table = jnp.concatenate(
            factors + leaf_factors + [jnp.zeros((128 - used, 128), jnp.float32)], axis=0
        )
        fac[...] = table.T
        mine = fac[pl.ds(pl.multiple_of(lax.rem(me, pack) * own_rows, own_rows), own_rows), :]
        for h in range(heads):
            at = slice(h * hd, (h + 1) * hd)
            sum_h = leaf_part[:, at] * mine[:, heads * n + h:heads * n + h + 1]
            for i in range(n):
                sum_h = sum_h + part_recv[i, :, at].astype(jnp.float32) * mine[:, h * n + i:h * n + i + 1]
            att_own[:, at] = sum_h.astype(jnp.bfloat16)

    with scope("attag"):
        send_all("node", lambda j: att_own, att_all, a_s, a_r)
        att_all[me] = att_own[...]
        in_copies[1].wait()
        settle(others(att_all, n), a_r)

    with scope("order"):
        mixed = nn_dot(order_ref[...], att_all[...].reshape(n * own_rows, span)).astype(jnp.bfloat16)
        for h in range(heads):
            for g in range(size):
                first = (h * size + g) * hd
                lhs[:, first:first + hd] = mixed[g * branches:(g + 1) * branches, h * hd:(h + 1) * hd]

    w_copies[0].wait()
    tiles, tile = pr_own.shape[0], pr_own.shape[2]

    def mp_peer(k):
        return lax.rem(mp_hi + k, mp_halves) * 2 + mp_lo

    def project(t, carry):
        at = pl.ds(pl.multiple_of(t * tile, tile), tile)
        value = nn_dot(lhs[...], ow[:, at])
        stream[:, at] = value
        pr_own[t] = value.astype(jnp.bfloat16)
        for k in range(1, mp_halves):
            peer = mp_peer(k)
            remote(
                pr_own.at[t], pr_hi.at[mp_hi, t], h_s, h_r.at[mp_hi, t], "mp", peer
            ).start()
        return carry

    def pair(t, carry):
        at = pl.ds(pl.multiple_of(t * tile, tile), tile)
        value = stream[:, at]
        for k in range(1, mp_halves):
            peer = mp_peer(k)
            at_hi = peer // 2
            remote(
                pr_own.at[t], pr_hi.at[at_hi, t], h_s, h_r.at[at_hi, t], "mp", peer
            ).wait_recv()
            value = value + pr_hi[at_hi, t].astype(jnp.float32)
        stream[:, at] = value
        pr_pair[t] = value.astype(jnp.bfloat16)
        remote(pr_pair.at[t], pr_lo.at[t], l_s, l_r.at[t], "mp", mp_partner).start()
        return carry

    def finish(t, squares):
        at = pl.ds(pl.multiple_of(t * tile, tile), tile)
        remote(pr_pair.at[t], pr_lo.at[t], l_s, l_r.at[t], "mp", mp_partner).wait_recv()
        value = stream[:, at] + pr_lo[t].astype(jnp.float32) + res_ref[:, at].astype(jnp.float32)
        stream[:, at] = value
        xg[:, at] = (value * gain_ref[:, at]).astype(jnp.bfloat16)
        return squares + jnp.sum(value * value, axis=1, keepdims=True)

    with scope("project"):
        lax.fori_loop(0, tiles, project, 0)
    with scope("prhi"):
        in_copies[2].wait()
        in_copies[3].wait()
        lax.fori_loop(0, tiles, pair, 0)
    with scope("prlo"):
        squares = lax.fori_loop(0, tiles, finish, jnp.zeros((branches, 1), jnp.float32))

    def early_sent():
        settle(others(qall, n), q_s)
        settle(others(part_recv, n), p_s)
        settle(others(st_recv, n), t_s)
        settle(others(att_all, n), a_s)

    with scope("wwait12"):
        w_copies[1].wait()
        w_copies[2].wait()

    def turn(i):
        down = jnp.where(owner_halves - 1 - i > hi, owner_halves - 1 - i, owner_halves - 2 - i)
        up = jnp.where(i < hi, i, i + 1)
        other = jnp.where(2 * hi >= owner_halves, up, down)
        return jnp.where((i == owner_halves - 1) & (hi < owner_halves), hi, other)

    def gate_up(j, off, count):
        at = pl.ds(pl.multiple_of(j * chunk + off, 128), count)
        return nn_dot(xg[...], gw[:, at]), nn_dot(xg[...], uw[:, at])

    def gx(k, s):
        at = pl.ds(subs[s][0], subs[s][1])
        return remote(
            gx_send.at[k, :, :, at], gx_recv.at[k, :, :, at], gx_s, gx_r.at[k, s], "node", partner
        )

    def gz(k, target, slot, s):
        at = pl.ds(subs[s][0], subs[s][1])
        return remote(
            gz_send.at[k, :, :, at], gz_recv.at[slot, :, :, at], gz_s, gz_r.at[slot, s],
            "node", target * 2 + lo,
        )

    line = halves == 4 and owner_halves == 4
    outer = (hi == 0) | (hi == 3)
    beside = hi + 1 - 2 * lax.rem(hi, 2)
    across_outer = jnp.where(hi < 2, 3, 0)
    across_inner = jnp.where(hi < 2, 2, 1)
    line_turn = (
        across_outer,
        jnp.where(outer, across_inner, beside),
        jnp.where(outer, beside, across_inner),
        hi,
    )

    def partner_side(s, k):
        off, count = subs[s]
        gate, upward = gate_up(k * 2 + 1 - lo, off, count)
        gx_send[k, 0, :, off:off + count] = gate.astype(jnp.bfloat16)
        gx_send[k, 1, :, off:off + count] = upward.astype(jnp.bfloat16)
        gx(k, s).start()

    def own_side(s, k):
        off, count = subs[s]
        at = slice(off, off + count)
        gate, upward = gate_up(k * 2 + lo, off, count)
        gx(k, s).wait_recv()
        gate = gate + gx_recv[k, 0, :, at].astype(jnp.float32)
        upward = upward + gx_recv[k, 1, :, at].astype(jnp.float32)
        return gate, upward

    def keep_own(s, gate, upward):
        at = slice(subs[s][0], subs[s][0] + subs[s][1])
        own_sum[0, :, at] = gate
        own_sum[1, :, at] = upward

    def pass_on(s, k, target, slot, gate, upward):
        at = slice(subs[s][0], subs[s][0] + subs[s][1])
        gz_send[k, 0, :, at] = gate.astype(jnp.bfloat16)
        gz_send[k, 1, :, at] = upward.astype(jnp.bfloat16)
        gz(k, target, slot, s).start()

    def own_line(s, p):
        at = slice(subs[s][0], subs[s][0] + subs[s][1])
        k = line_turn[p]
        gate, upward = own_side(s, k)
        if p == 3:
            keep_own(s, gate, upward)
        elif p == 1:
            pass_on(s, k, beside, jnp.where(outer, 1, 2), gate, upward)
        else:
            held = p // 2

            @pl.when(outer)
            def _():
                pass_on(s, k, beside, p, gate, upward)

            @pl.when(jnp.logical_not(outer))
            def _():
                gz(k, beside, held, s).wait_recv()
                pass_on(
                    s, k, k, 3,
                    gate + gz_recv[held, 0, :, at].astype(jnp.float32),
                    upward + gz_recv[held, 1, :, at].astype(jnp.float32),
                )

    def own_direct(s, k):
        gate, upward = own_side(s, k)
        pl.when(k == hi)(lambda: keep_own(s, gate, upward))
        pl.when(k != hi)(lambda: pass_on(s, k, k, hi, gate, upward))

    def partner_turns(i, carry):
        for s in range(len(subs)):
            partner_side(s, turn(i))
        return carry

    def own_turns(i, carry):
        for s in range(len(subs)):
            own_direct(s, turn(i))
        return carry

    def act_z(k, s, owner, sem_at):
        at = pl.ds(subs[s][0], subs[s][1])
        return remote(
            act_all.at[owner, :, at], act_all.at[owner, :, at], cz_s, cz_r.at[sem_at, s],
            "node", k * 2 + lo,
        )

    def act_x(k, s, side):
        owner = k * 2 + side
        at = pl.ds(subs[s][0], subs[s][1])
        return remote(
            act_all.at[owner, :, at], act_all.at[owner, :, at], cx_s, cx_r.at[k, s], "node", partner
        )

    def other_halves(fn):
        def body(i, carry):
            down = jnp.where(halves - 1 - i > hi, halves - 1 - i, halves - 2 - i)
            fn(jnp.where(2 * hi >= halves, jnp.where(i < hi, i, i + 1), down))
            return carry

        lax.fori_loop(0, halves - 1, lambda i, carry: body(halves - 2 - i, carry), 0)

    def norm_scale():
        settle(others(sq_all, n), s_r)
        total = sq_all[0]
        for k in range(1, n):
            total = total + sq_all[k]
        mean = total / (width * n)
        sq_own_scale[...] = jnp.concatenate([lax.rsqrt(mean + norm_eps)] * 16, axis=0).T

    def owner_work(s):
        off, count = subs[s]
        at = slice(off, off + count)
        root_mean = sq_own_scale[0:branches, 0:1]

        def add(k, carry):
            return (
                carry[0] + gz_recv[k, 0, :, at].astype(jnp.float32),
                carry[1] + gz_recv[k, 1, :, at].astype(jnp.float32),
            )

        gate, upward = own_sum[0, :, at], own_sum[1, :, at]
        if line:
            for slot in (2, 3):
                gz(0, beside, slot, s).wait_recv()
                gate, upward = add(slot, (gate, upward))
        else:
            other_halves(lambda k: gz(0, k, k, s).wait_recv())
            gate, upward = lax.fori_loop(
                1, halves, lambda i, carry: add(lax.rem(hi + i, halves), carry), (gate, upward)
            )
        gate, upward = gate * root_mean, upward * root_mean
        act_all[me, :, at] = (gate / (1.0 + jnp.exp(-gate)) * upward).astype(jnp.bfloat16)
        act_x(hi, s, lo).start()
        other_halves(lambda k: act_z(k, s, me, hi).start())

    def own_act(s):
        if owners == n:
            owner_work(s)
        else:
            pl.when(me < owners)(functools.partial(owner_work, s))

    def down(owner, s):
        off, count = subs[s]
        at = pl.ds(pl.multiple_of(owner * chunk + off, 128), count)
        acc[...] += nn_dot(act_all[owner, :, off:off + count], dw[at, :])

    def forward(i, carry):
        k = turn(owner_halves - 1 - i)
        for s in range(steps):
            @pl.when(k != hi)
            def _():
                act_z(k, s, k * 2 + lo, k).wait_recv()
                act_x(k, s, lo).start()

        for s in range(steps):
            down(k * 2 + lo, s)
        return carry

    def from_partner(i, carry):
        k = turn(owner_halves - 1 - i)
        for s in range(steps):
            act_x(k, s, 1 - lo).wait_recv()
            down(k * 2 + 1 - lo, s)
        return carry

    steps = len(subs)
    acc[...] = jnp.zeros(acc.shape, jnp.float32)
    with scope("gupartner"):
        if line:
            for p in range(4):
                for s in range(steps):
                    partner_side(s, line_turn[p])
        else:
            lax.fori_loop(0, owner_halves, partner_turns, 0)
    with scope("sqsend"):
        sq_own[...] = to_lanes([squares])[0:8]
        send_all("node", lambda j: sq_own, sq_all, s_s, s_r)
        sq_all[me] = sq_own[...]
        early_sent()
    if line:
        for p in range(4):
            for s in range(steps):
                with scope(f"own{p}{s}"):
                    own_line(s, p)
    else:
        lax.fori_loop(0, owner_halves, own_turns, 0)
    with scope("norm"):
        norm_scale()
    w_copies[3].wait()
    for s in range(steps):
        with scope(f"act{s}"):
            own_act(s)
    with scope("forward"):
        lax.fori_loop(0, owner_halves, forward, 0)
    with scope("frompartner"):
        lax.fori_loop(0, owner_halves, from_partner, 0)

    rows_out = out_ref.shape[0]
    with scope("dnx"):
        for k in range(mp):
            dn_send[k] = acc[k * rows_out:(k + 1) * rows_out, :].astype(jnp.bfloat16)
        send_all("mp", lambda j: dn_send.at[j], dn_recv, d_s, d_r)
        dn_recv[mpi] = dn_send[mpi]
        settle(others(sq_all, n), s_s)
        for _ in range(1, mp_halves):
            settle(pr_own, h_s)
        settle(pr_pair, l_s)
        settle(gx_send, gx_s)
        settle(act_all.at[pl.ds(0, owner_halves)], cx_s)
        if owners == n:
            settle(others(gz_send, owner_halves), gz_s)
            settle(act_all.at[pl.ds(0, halves - 1)], cz_s)
        else:
            owning = hi < owner_halves
            pl.when(owning)(lambda: settle(others(gz_send, owner_halves), gz_s))
            pl.when(owning)(lambda: settle(act_all.at[pl.ds(0, halves - 1)], cz_s))
            pl.when(jnp.logical_not(owning))(lambda: settle(gz_send, gz_s))
        settle(others(dn_recv, mp), d_r)
        total = dn_recv[0].astype(jnp.float32)
        for k in range(1, mp):
            total = total + dn_recv[k].astype(jnp.float32)
        own = stream[pl.ds(pl.multiple_of(mpi * rows_out, rows_out), rows_out), :]
        out_ref[...] = (own + total).astype(jnp.bfloat16)

    with scope("drain"):
        settle(others(dn_recv, mp), d_s)


def on_device(
    n, mp,
    queries, root_keys, root_values, mid_keys, mid_values, leaf_keys, leaf_values,
    mid_length, leaf_length, branch_mid, residual, norm_gain,
    out_weight, gate_weight, up_weight, down_weight,
):
    owned, local_heads, hd = queries.shape
    heads = root_keys.shape[1]
    size = local_heads // heads
    own_rows = owned * size
    branches = owned * n
    width = residual.shape[1]
    hidden = gate_weight.shape[1]
    lane_tiles = hidden // 128
    owners = max(k for k in range(2, n + 1, 2) if lane_tiles % k == 0)
    chunk = hidden // owners
    first = (chunk // 128 + 1) // 2 * 128
    subs = ((0, first), (first, chunk - first)) if first < chunk else ((0, chunk),)
    mid_slots = mid_keys.shape[1]
    leaf_slots = leaf_keys.shape[1]
    local_mids = mid_keys.shape[0]
    halves, owner_halves, mp_halves = n // 2, owners // 2, mp // 2
    group = max(1, min(n, ROWS // own_rows))
    pack = min(group, 128 // own_rows)
    tile = math.gcd(width, 256)
    tiles = width // tile

    order = np.zeros((branches * size, branches * size), np.float32)
    at = np.arange(branches * size)
    order[(at % size) * branches + at // size, at] = 1.0

    flat = [
        a.reshape(-1, hd)
        for a in (root_keys, root_values, mid_keys, mid_values, leaf_keys, leaf_values)
    ]
    kv_rows = flat[0].shape[0] + flat[2].shape[0] + flat[4].shape[0]
    span = heads * hd
    bf, f32 = jnp.bfloat16, jnp.float32
    dma = pltpu.SemaphoreType.DMA
    vmem = pl.BlockSpec(memory_space=pltpu.VMEM)
    smem = pl.BlockSpec(memory_space=pltpu.SMEM)
    hbm = pl.BlockSpec(memory_space=pl.ANY)
    rows_out = branches // mp
    scratch = [
        pltpu.VMEM((owned, local_heads, hd), bf),
        pltpu.VMEM(order.shape, bf),
        pltpu.VMEM((branches, width), bf),
        pltpu.VMEM((1, width), f32),
        pltpu.VMEM((kv_rows, span), bf),
        pltpu.VMEM((kv_rows, span), bf),
        pltpu.VMEM(out_weight.shape, bf),
        pltpu.VMEM(gate_weight.shape, bf),
        pltpu.VMEM(up_weight.shape, bf),
        pltpu.VMEM(down_weight.shape, bf),
        pltpu.VMEM((own_rows, span), bf),
        pltpu.VMEM((n, own_rows, span), bf),
        pltpu.VMEM((n, own_rows, span), bf),
        pltpu.VMEM((n, own_rows, span), bf),
        pltpu.VMEM((n // pack, 8, 128), f32),
        pltpu.VMEM((n, 8, 128), f32),
        pltpu.VMEM((own_rows, span), f32),
        pltpu.VMEM((128, 128), f32),
        pltpu.VMEM((own_rows, span), bf),
        pltpu.VMEM((n, own_rows, span), bf),
        pltpu.VMEM((branches, local_heads * hd), bf),
        pltpu.VMEM((tiles, branches, tile), bf),
        pltpu.VMEM((mp_halves, tiles, branches, tile), bf),
        pltpu.VMEM((tiles, branches, tile), bf),
        pltpu.VMEM((tiles, branches, tile), bf),
        pltpu.VMEM((branches, width), f32),
        pltpu.VMEM((8, 128), f32),
        pltpu.VMEM((n, 8, 128), f32),
        pltpu.VMEM((128, 128), f32),
        pltpu.VMEM((branches, width), bf),
        pltpu.VMEM((owner_halves, 2, branches, chunk), bf),
        pltpu.VMEM((owner_halves, 2, branches, chunk), bf),
        pltpu.VMEM((2, branches, chunk), f32),
        pltpu.VMEM((owner_halves, 2, branches, chunk), bf),
        pltpu.VMEM((halves, 2, branches, chunk), bf),
        pltpu.VMEM((owners, branches, chunk), bf),
        pltpu.VMEM((branches, width), f32),
        pltpu.VMEM((mp, rows_out, width), bf),
        pltpu.VMEM((mp, rows_out, width), bf),
        dma((4,)),
        dma((2,)),
        dma((4,)),
        dma(()),
        dma((n // group,)),
    ] + [dma(())] * 8 + [
        dma(()),
        dma((mp_halves, tiles)),
        dma(()),
        dma((tiles,)),
        dma(()),
        dma((owner_halves, len(subs))),
        dma(()),
        dma((halves, len(subs))),
        dma(()),
        dma((owner_halves, len(subs))),
        dma(()),
        dma((owner_halves, len(subs))),
        dma(()),
        dma(()),
    ]
    scale2 = hd ** -0.5 * math.log2(math.e)
    return pl.pallas_call(
        functools.partial(
            layer_kernel, n, mp, owners, scale2, local_mids, mid_slots, leaf_slots, size, subs
        ),
        out_shape=pltpu.VMEM((rows_out, width), bf),
        in_specs=[smem] * 3 + [hbm] * 14,
        out_specs=vmem,
        scratch_shapes=scratch,
        compiler_params=pltpu.CompilerParams(
            collective_id=0, has_side_effects=True, vmem_limit_bytes=66900000
        ),
    )(
        branch_mid.reshape(-1), mid_length, leaf_length,
        queries, jnp.asarray(order, bf), residual, norm_gain[None, :],
        *flat, out_weight, gate_weight, up_weight, down_weight,
    )


def solution(mesh):
    in_specs = (
        P("node", "mp", None),
        P("node", "mp", None),
        P("node", "mp", None),
        P("node", None, "mp", None),
        P("node", None, "mp", None),
        P("node", None, "mp", None),
        P("node", None, "mp", None),
        P(),
        P("node"),
        P(),
        P(None, "node"),
        P("node"),
        P("mp", "node"),
        P("node", "mp"),
        P("node", "mp"),
        P("mp", "node"),
    )
    body = functools.partial(on_device, mesh.shape["node"], mesh.shape["mp"])
    return jax.shard_map(
        body, mesh=mesh, in_specs=in_specs, out_specs=P("mp", "node"), check_vma=False
    )
```

```python
import functools
import math
from contextlib import nullcontext as scope

import jax
import jax.numpy as jnp
import numpy as np
from jax import lax
from jax.experimental import pallas as pl
from jax.experimental.pallas import tpu as pltpu
from jax.sharding import PartitionSpec as P

norm_eps = 1e-05
masked_score = -1e30
MESH = pl.DeviceIdType.MESH
ROWS = 256
PIECES = 2


def nt_dot(a, b):
    return lax.dot_general(a, b, (((1,), (1,)), ((), ())), preferred_element_type=jnp.float32)


def nn_dot(a, b):
    return jnp.dot(a, b, preferred_element_type=jnp.float32)


def to_lanes(columns):
    rows = columns[0].shape[0]
    lane = lax.broadcasted_iota(jnp.int32, (rows, 128), 1)
    grid = jnp.zeros((rows, 128), jnp.float32)
    for k, column in enumerate(columns):
        grid = jnp.where(lane == k, column, grid)
    if rows < 128:
        grid = jnp.concatenate([grid] * (128 // rows), axis=0)
    return grid.T


def layer_kernel(
    n, mp, owners, scale2, local_mids, mid_slots, leaf_slots, size, subs,
    mid_of_hbm, mid_len_hbm, leaf_len_hbm, q_hbm, order_hbm, res_hbm, gain_hbm,
    rk_hbm, rv_hbm, mk_hbm, mv_hbm, lk_hbm, lv_hbm, ow_hbm, gw_hbm, uw_hbm, dw_hbm,
    out_ref,
    mid_of, mid_len, leaf_len, q_raw, order_ref, res_ref, gain_ref, keys, values, ow, gw, uw, dw,
    q_own, qall, part_send, part_recv, st_send, st_recv, leaf_part, fac, att_own, att_all, lhs,
    pr_own, pr_hi, pr_pair, pr_lo, stream, sq_own, sq_all, sq_own_scale, xg,
    gx_send, gx_recv, own_sum, gz_send, gz_recv, act_all, acc, dn_send, dn_recv,
    in_sem, kv_sem, w_sem, q_s, q_r, p_s, p_r, t_s, t_r, a_s, a_r, s_s, s_r,
    h_s, h_r, l_s, l_r, gx_s, gx_r, gz_s, gz_r, cz_s, cz_r, cx_s, cx_r, d_s, d_r,
):
    me = lax.axis_index("node")
    mpi = lax.axis_index("mp")
    owned, local_heads, hd = q_raw.shape
    heads = local_heads // size
    own_rows = owned * size
    span = heads * hd
    chunk = act_all.shape[2]
    branches, width = stream.shape
    root = rk_hbm.shape[0]
    mids = mk_hbm.shape[0]
    shared = root + mids
    lo, hi = lax.rem(me, 2), me // 2
    partner = me + 1 - 2 * lo
    halves = n // 2
    owner_halves = owners // 2
    mp_lo, mp_hi = lax.rem(mpi, 2), mpi // 2
    mp_partner = mpi + 1 - 2 * mp_lo
    mp_halves = mp // 2

    in_copies = [
        pltpu.make_async_copy(src, dst, in_sem.at[k])
        for k, (src, dst) in enumerate(
            (
                (q_hbm, q_raw), (order_hbm, order_ref), (res_hbm, res_ref), (gain_hbm, gain_ref),
                (mid_of_hbm, mid_of), (mid_len_hbm, mid_len), (leaf_len_hbm, leaf_len),
            )
        )
    ]
    in_copies[0].start()
    barrier = pltpu.get_barrier_semaphore()

    def greet(axis, here, count):
        def body(i, carry):
            pl.semaphore_signal(
                barrier, inc=1, device_id={axis: lax.rem(here + i, count)}, device_id_type=MESH
            )
            return carry

        lax.fori_loop(1, count, body, 0)

    greet("node", me, n)
    greet("mp", mpi, mp)
    for side, (dst, parts) in enumerate(
        ((keys, (rk_hbm, mk_hbm, lk_hbm)), (values, (rv_hbm, mv_hbm, lv_hbm)))
    ):
        start = 0
        for src in parts:
            rows = src.shape[0]
            pltpu.make_async_copy(
                src, dst.at[pl.ds(start, rows), pl.ds(0, hd)], kv_sem.at[side]
            ).start()
            start += rows
    for copy in in_copies[1:]:
        copy.start()
    w_copies = [
        pltpu.make_async_copy(src, dst, w_sem.at[k])
        for k, (src, dst) in enumerate(((ow_hbm, ow), (gw_hbm, gw), (uw_hbm, uw), (dw_hbm, dw)))
    ]

    def remote(src, dst, send, recv, axis, peer):
        return pltpu.make_async_remote_copy(
            src_ref=src, dst_ref=dst, send_sem=send, recv_sem=recv,
            device_id={axis: peer}, device_id_type=MESH,
        )

    def peers(axis, fn):
        here, count = (me, n) if axis == "node" else (mpi, mp)

        def body(i, carry):
            fn(lax.rem(here + i, count))
            return carry

        lax.fori_loop(1, count, body, 0)

    def send_all(axis, src, dst, send, recv):
        here = me if axis == "node" else mpi
        peers(axis, lambda j: remote(src(j), dst.at[here], send, recv, axis, j).start())

    def settle(ref, sem):
        pltpu.make_async_copy(ref, ref, sem).wait()

    def others(ref, count):
        return ref.at[pl.ds(0, count - 1)]

    with scope("qprep"):
        in_copies[0].wait()
        raw_q = q_raw[...].astype(jnp.float32)
        for h in range(heads):
            q_own[:, h * hd:(h + 1) * hd] = (
                raw_q[:, h * size:(h + 1) * size, :].reshape(own_rows, hd).astype(jnp.bfloat16)
            )
        qall[me] = q_own[...]

    with scope("barrier"):
        pl.semaphore_wait(barrier, n - 1 + mp - 1)
    group = max(1, min(n, ROWS // own_rows))
    groups = n // group

    def send_query(j):
        remote(q_own, qall.at[me], q_s, q_r.at[me // group], "node", j).start()

    def send_near(k, carry):
        send_query(me // group * group + lax.rem(me + k, group))
        return carry

    def send_far(k, carry):
        send_query(lax.rem(me // group * group + k, n))
        return carry

    lax.fori_loop(1, group, send_near, 0)
    lax.fori_loop(group, n, send_far, 0)

    with scope("kvwait"):
        for copy in in_copies[4:]:
            copy.wait()
        for side, ref in enumerate((keys, values)):
            arrived = ref.at[:, pl.ds(0, hd)]
            pltpu.make_async_copy(arrived, arrived, kv_sem.at[side]).wait()
    for copy in w_copies:
        copy.start()

    block = math.gcd(512, math.gcd(shared, leaf_slots * heads))
    row = lax.broadcasted_iota(jnp.int32, (block, hd), 0)
    keep = [(lax.rem(row, heads) == h).astype(jnp.float32).astype(jnp.bfloat16) for h in range(heads)]

    def spread(i, carry):
        at = pl.ds(pl.multiple_of(i * block, block), block)
        for ref in (keys, values):
            mixed = ref[at, 0:hd]
            for h in range(heads):
                ref[at, h * hd:(h + 1) * hd] = mixed * keep[h]
        return carry

    with scope("spread"):
        lax.fori_loop(0, shared // block, spread, 0)

    def attend_rows(query, spans, seen):
        rows = query.shape[0]
        lane = lax.broadcasted_iota(jnp.int32, (rows, 128), 1)
        mine = [lax.rem(lane, heads) == h for h in range(heads)]

        def mix(columns):
            mixed = jnp.broadcast_to(columns[0], lane.shape)
            for h in range(1, heads):
                mixed = jnp.where(mine[h], columns[h], mixed)
            return mixed

        peaks, total, weighted = None, None, None
        for start, count in spans:
            scores = nt_dot(query, keys[start:start + count, :])
            parts = [
                seen(start + k, scores[:, k:k + 128], lane) for k in range(0, count, 128)
            ]
            top = functools.reduce(jnp.maximum, parts)
            now = [
                jnp.max(jnp.where(mine[h], top, -jnp.inf), axis=1, keepdims=True) for h in range(heads)
            ]
            if peaks is not None:
                now = [jnp.maximum(a, b) for a, b in zip(peaks, now)]
                shrink = [jnp.exp2((a - b) * scale2) for a, b in zip(peaks, now)]
                total = total * mix(shrink)
                weighted = weighted * jnp.concatenate(
                    [jnp.broadcast_to(a, (rows, hd)) for a in shrink], axis=1
                )
            peaks = now
            mixed = mix(peaks)
            rounded = []
            for part in parts:
                part = jnp.exp2((part - mixed) * scale2)
                total = part if total is None else total + part
                rounded.append(part.astype(jnp.bfloat16))
            product = nn_dot(jnp.concatenate(rounded, axis=1), values[start:start + count, :])
            weighted = product if weighted is None else weighted + product
        totals = [
            jnp.sum(jnp.where(mine[h], total, 0.0), axis=1, keepdims=True) for h in range(heads)
        ]
        return peaks, totals, weighted

    pack = min(group, 128 // own_rows)
    blocks = group // pack
    rows = group * own_rows
    group_branches = group * owned
    piece = math.gcd(2048, math.gcd(root, mids))

    def attend(i, carry):
        g = lax.rem(me // group + i, groups)

        def each(fn):
            for k in range(group):
                j = g * group + lax.rem(me - g * group + group // 2 + k + group, group)
                pl.when(j != me)(functools.partial(fn, j))

        pl.when(g == me // group)(lambda: settle(qall.at[pl.ds(0, group - 1)], q_r.at[g]))
        if groups > 1:
            pl.when(g != me // group)(lambda: settle(qall.at[pl.ds(0, group)], q_r.at[g]))
        lows, highs = [], []
        for b in range(group_branches):
            mid = mid_of[g * group_branches + b]
            local = mid - me * local_mids
            here = (local >= 0) & (local < local_mids)
            low = local * (mid_slots * heads)
            highs.append(jnp.full((size, 128), jnp.where(here, low + mid_len[mid] * heads, 0), jnp.int32))
            lows.append(jnp.full((size, 128), jnp.where(here, low, 0), jnp.int32))
        low, high = jnp.concatenate(lows, axis=0), jnp.concatenate(highs, axis=0)
        query = qall[pl.ds(g * group, group)].reshape(rows, span)

        def seen(start, part, lane):
            if start < root:
                return part
            column = lane + (start - root)
            kept = column < high
            if local_mids > 1:
                kept = kept & (column >= low)
            return jnp.where(kept, part, masked_score)

        tops, totals, weighted = attend_rows(
            query, [(start, piece) for start in range(0, shared, piece)], seen
        )
        part_send[pl.ds(g * group, group)] = weighted.astype(jnp.bfloat16).reshape(group, own_rows, span)
        columns = tops + totals
        for k in range(blocks):
            at = slice(k * pack * own_rows, (k + 1) * pack * own_rows)
            st_send[g * blocks + k] = to_lanes([column[at] for column in columns])[0:8]

        def send(j):
            remote(part_send.at[j], part_recv.at[me], p_s, p_r, "node", j).start()
            remote(st_send.at[j // pack], st_recv.at[me], t_s, t_r, "node", j).start()

        each(send)
        return carry

    with scope("attend"):
        lax.fori_loop(0, groups, attend, 0)
    part_recv[me] = part_send[me]
    st_recv[me] = st_send[me // pack]

    with scope("leaf"):
        lax.fori_loop(shared // block, keys.shape[0] // block, spread, 0)
        leaf_rows = leaf_slots * heads
        stats = []
        for b in range(owned):
            start = shared + b * leaf_rows
            tops, totals, weighted = attend_rows(
                q_own[b * size:(b + 1) * size, :],
                [(start, leaf_rows)],
                lambda at, part, lane: jnp.where(
                    lane + (at - start) < leaf_len[b] * heads, part, masked_score
                ),
            )
            leaf_part[b * size:(b + 1) * size, :] = weighted
            stats.append(tops + totals)
        leaf_stats = to_lanes([
            jnp.concatenate([stats[b][k] for b in range(owned)], axis=0) for k in range(2 * heads)
        ])[0:8]

    with scope("partx"):
        settle(others(part_recv, n), p_r)
        settle(others(st_recv, n), t_r)

    with scope("merge"):
        factors = []
        leaf_factors = []
        for h in range(heads):
            peak = jnp.concatenate([st_recv[i, h:h + 1, :] for i in range(n)], axis=0)
            total = jnp.concatenate([st_recv[i, heads + h:heads + h + 1, :] for i in range(n)], axis=0)
            leaf_peak, leaf_total = leaf_stats[h:h + 1], leaf_stats[heads + h:heads + h + 1]
            top = jnp.maximum(jnp.max(peak, axis=0, keepdims=True), leaf_peak)
            scale, leaf_scale = jnp.exp2((peak - top) * scale2), jnp.exp2((leaf_peak - top) * scale2)
            whole = jnp.sum(total * scale, axis=0, keepdims=True) + leaf_total * leaf_scale
            factors.append(scale / whole)
            leaf_factors.append(leaf_scale / whole)
        used = heads * n + heads
        table = jnp.concatenate(
            factors + leaf_factors + [jnp.zeros((128 - used, 128), jnp.float32)], axis=0
        )
        fac[...] = table.T
        mine = fac[pl.ds(pl.multiple_of(lax.rem(me, pack) * own_rows, own_rows), own_rows), :]
        for h in range(heads):
            at = slice(h * hd, (h + 1) * hd)
            sum_h = leaf_part[:, at] * mine[:, heads * n + h:heads * n + h + 1]
            for i in range(n):
                sum_h = sum_h + part_recv[i, :, at].astype(jnp.float32) * mine[:, h * n + i:h * n + i + 1]
            att_own[:, at] = sum_h.astype(jnp.bfloat16)

    with scope("attag"):
        send_all("node", lambda j: att_own, att_all, a_s, a_r)
        att_all[me] = att_own[...]
        in_copies[1].wait()
        settle(others(att_all, n), a_r)

    with scope("order"):
        mixed = nn_dot(order_ref[...], att_all[...].reshape(n * own_rows, span)).astype(jnp.bfloat16)
        for h in range(heads):
            for g in range(size):
                first = (h * size + g) * hd
                lhs[:, first:first + hd] = mixed[g * branches:(g + 1) * branches, h * hd:(h + 1) * hd]

    w_copies[0].wait()
    tiles, tile = pr_own.shape[0], pr_own.shape[2]

    def mp_peer(k):
        return lax.rem(mp_hi + k, mp_halves) * 2 + mp_lo

    def project(t, carry):
        at = pl.ds(pl.multiple_of(t * tile, tile), tile)
        value = nn_dot(lhs[...], ow[:, at])
        stream[:, at] = value
        pr_own[t] = value.astype(jnp.bfloat16)
        for k in range(1, mp_halves):
            peer = mp_peer(k)
            remote(
                pr_own.at[t], pr_hi.at[mp_hi, t], h_s, h_r.at[mp_hi, t], "mp", peer
            ).start()
        return carry

    def pair(t, carry):
        at = pl.ds(pl.multiple_of(t * tile, tile), tile)
        value = stream[:, at]
        for k in range(1, mp_halves):
            peer = mp_peer(k)
            at_hi = peer // 2
            remote(
                pr_own.at[t], pr_hi.at[at_hi, t], h_s, h_r.at[at_hi, t], "mp", peer
            ).wait_recv()
            value = value + pr_hi[at_hi, t].astype(jnp.float32)
        stream[:, at] = value
        pr_pair[t] = value.astype(jnp.bfloat16)
        remote(pr_pair.at[t], pr_lo.at[t], l_s, l_r.at[t], "mp", mp_partner).start()
        return carry

    def finish(t, squares):
        at = pl.ds(pl.multiple_of(t * tile, tile), tile)
        remote(pr_pair.at[t], pr_lo.at[t], l_s, l_r.at[t], "mp", mp_partner).wait_recv()
        value = stream[:, at] + pr_lo[t].astype(jnp.float32) + res_ref[:, at].astype(jnp.float32)
        stream[:, at] = value
        xg[:, at] = (value * gain_ref[:, at]).astype(jnp.bfloat16)
        return squares + jnp.sum(value * value, axis=1, keepdims=True)

    with scope("project"):
        lax.fori_loop(0, tiles, project, 0)
    with scope("prhi"):
        in_copies[2].wait()
        in_copies[3].wait()
        lax.fori_loop(0, tiles, pair, 0)
    with scope("prlo"):
        squares = lax.fori_loop(0, tiles, finish, jnp.zeros((branches, 1), jnp.float32))

    def early_sent():
        settle(others(qall, n), q_s)
        settle(others(part_recv, n), p_s)
        settle(others(st_recv, n), t_s)
        settle(others(att_all, n), a_s)

    with scope("wwait12"):
        w_copies[1].wait()
        w_copies[2].wait()

    def turn(i):
        down = jnp.where(owner_halves - 1 - i > hi, owner_halves - 1 - i, owner_halves - 2 - i)
        up = jnp.where(i < hi, i, i + 1)
        other = jnp.where(2 * hi >= owner_halves, up, down)
        return jnp.where((i == owner_halves - 1) & (hi < owner_halves), hi, other)

    def gate_up(j, off, count):
        at = pl.ds(pl.multiple_of(j * chunk + off, 128), count)
        return nn_dot(xg[...], gw[:, at]), nn_dot(xg[...], uw[:, at])

    def gx(k, s):
        at = pl.ds(subs[s][0], subs[s][1])
        return remote(
            gx_send.at[k, :, :, at], gx_recv.at[k, :, :, at], gx_s, gx_r.at[k, s], "node", partner
        )

    def gz(k, target, slot, s):
        at = pl.ds(subs[s][0], subs[s][1])
        return remote(
            gz_send.at[k, :, :, at], gz_recv.at[slot, :, :, at], gz_s, gz_r.at[slot, s],
            "node", target * 2 + lo,
        )

    line = halves == 4 and owner_halves == 4
    outer = (hi == 0) | (hi == 3)
    beside = hi + 1 - 2 * lax.rem(hi, 2)
    across_outer = jnp.where(hi < 2, 3, 0)
    across_inner = jnp.where(hi < 2, 2, 1)
    line_turn = (
        across_outer,
        jnp.where(outer, across_inner, beside),
        jnp.where(outer, beside, across_inner),
        hi,
    )

    def partner_side(s, k):
        off, count = subs[s]
        gate, upward = gate_up(k * 2 + 1 - lo, off, count)
        gx_send[k, 0, :, off:off + count] = gate.astype(jnp.bfloat16)
        gx_send[k, 1, :, off:off + count] = upward.astype(jnp.bfloat16)
        gx(k, s).start()

    def own_side(s, k):
        off, count = subs[s]
        at = slice(off, off + count)
        gate, upward = gate_up(k * 2 + lo, off, count)
        gx(k, s).wait_recv()
        gate = gate + gx_recv[k, 0, :, at].astype(jnp.float32)
        upward = upward + gx_recv[k, 1, :, at].astype(jnp.float32)
        return gate, upward

    def keep_own(s, gate, upward):
        at = slice(subs[s][0], subs[s][0] + subs[s][1])
        own_sum[0, :, at] = gate
        own_sum[1, :, at] = upward

    def pass_on(s, k, target, slot, gate, upward):
        at = slice(subs[s][0], subs[s][0] + subs[s][1])
        gz_send[k, 0, :, at] = gate.astype(jnp.bfloat16)
        gz_send[k, 1, :, at] = upward.astype(jnp.bfloat16)
        gz(k, target, slot, s).start()

    def own_line(s, p):
        at = slice(subs[s][0], subs[s][0] + subs[s][1])
        k = line_turn[p]
        gate, upward = own_side(s, k)
        if p == 3:
            keep_own(s, gate, upward)
        elif p == 1:
            pass_on(s, k, beside, jnp.where(outer, 1, 2), gate, upward)
        else:
            held = p // 2

            @pl.when(outer)
            def _():
                pass_on(s, k, beside, p, gate, upward)

            @pl.when(jnp.logical_not(outer))
            def _():
                gz(k, beside, held, s).wait_recv()
                pass_on(
                    s, k, k, 3,
                    gate + gz_recv[held, 0, :, at].astype(jnp.float32),
                    upward + gz_recv[held, 1, :, at].astype(jnp.float32),
                )

    def own_direct(s, k):
        gate, upward = own_side(s, k)
        pl.when(k == hi)(lambda: keep_own(s, gate, upward))
        pl.when(k != hi)(lambda: pass_on(s, k, k, hi, gate, upward))

    def partner_turns(i, carry):
        for s in range(len(subs)):
            partner_side(s, turn(i))
        return carry

    def own_turns(i, carry):
        for s in range(len(subs)):
            own_direct(s, turn(i))
        return carry

    def act_z(k, s, owner, sem_at):
        at = pl.ds(subs[s][0], subs[s][1])
        return remote(
            act_all.at[owner, :, at], act_all.at[owner, :, at], cz_s, cz_r.at[sem_at, s],
            "node", k * 2 + lo,
        )

    def act_x(k, s, side):
        owner = k * 2 + side
        at = pl.ds(subs[s][0], subs[s][1])
        return remote(
            act_all.at[owner, :, at], act_all.at[owner, :, at], cx_s, cx_r.at[k, s], "node", partner
        )

    def other_halves(fn):
        def body(i, carry):
            down = jnp.where(halves - 1 - i > hi, halves - 1 - i, halves - 2 - i)
            fn(jnp.where(2 * hi >= halves, jnp.where(i < hi, i, i + 1), down))
            return carry

        lax.fori_loop(0, halves - 1, lambda i, carry: body(halves - 2 - i, carry), 0)

    def norm_scale():
        settle(others(sq_all, n), s_r)
        total = sq_all[0]
        for k in range(1, n):
            total = total + sq_all[k]
        mean = total / (width * n)
        sq_own_scale[...] = jnp.concatenate([lax.rsqrt(mean + norm_eps)] * 16, axis=0).T

    def owner_work(s):
        off, count = subs[s]
        at = slice(off, off + count)
        root_mean = sq_own_scale[0:branches, 0:1]

        def add(k, carry):
            return (
                carry[0] + gz_recv[k, 0, :, at].astype(jnp.float32),
                carry[1] + gz_recv[k, 1, :, at].astype(jnp.float32),
            )

        gate, upward = own_sum[0, :, at], own_sum[1, :, at]
        if line:
            for slot in (2, 3):
                gz(0, beside, slot, s).wait_recv()
                gate, upward = add(slot, (gate, upward))
        else:
            other_halves(lambda k: gz(0, k, k, s).wait_recv())
            gate, upward = lax.fori_loop(
                1, halves, lambda i, carry: add(lax.rem(hi + i, halves), carry), (gate, upward)
            )
        gate, upward = gate * root_mean, upward * root_mean
        act_all[me, :, at] = (gate / (1.0 + jnp.exp(-gate)) * upward).astype(jnp.bfloat16)
        act_x(hi, s, lo).start()
        other_halves(lambda k: act_z(k, s, me, hi).start())

    def own_act(s):
        if owners == n:
            owner_work(s)
        else:
            pl.when(me < owners)(functools.partial(owner_work, s))

    def down(owner, s):
        off, count = subs[s]
        at = pl.ds(pl.multiple_of(owner * chunk + off, 128), count)
        acc[...] += nn_dot(act_all[owner, :, off:off + count], dw[at, :])

    def forward_turns(i, carry):
        k = turn(owner_halves - 1 - i)
        for s in range(steps):
            @pl.when(k != hi)
            def _():
                act_z(k, s, k * 2 + lo, k).wait_recv()
                act_x(k, s, lo).start()

        for s in range(steps):
            down(k * 2 + lo, s)
        return carry

    def partner_acts(i, carry):
        k = turn(owner_halves - 1 - i)
        for s in range(steps):
            act_x(k, s, 1 - lo).wait_recv()
            down(k * 2 + 1 - lo, s)
        return carry

    steps = len(subs)
    acc[...] = jnp.zeros(acc.shape, jnp.float32)
    with scope("gupartner"):
        if line:
            for p in range(4):
                for s in range(steps):
                    partner_side(s, line_turn[p])
        else:
            lax.fori_loop(0, owner_halves, partner_turns, 0)
    with scope("sqsend"):
        sq_own[...] = to_lanes([squares])[0:8]
        send_all("node", lambda j: sq_own, sq_all, s_s, s_r)
        sq_all[me] = sq_own[...]
        early_sent()
    if line:
        for p in range(4):
            if p == 3:
                norm_scale()
            for s in range(steps):
                with scope(f"own{p}{s}"):
                    own_line(s, p)
    else:
        lax.fori_loop(0, owner_halves, own_turns, 0)
        norm_scale()
    w_copies[3].wait()
    for s in range(steps):
        with scope(f"act{s}"):
            own_act(s)
    with scope("forward"):
        lax.fori_loop(0, owner_halves, forward_turns, 0)
    with scope("frompartner"):
        lax.fori_loop(0, owner_halves, partner_acts, 0)

    rows_out = out_ref.shape[0]
    with scope("dnx"):
        for k in range(mp):
            dn_send[k] = acc[k * rows_out:(k + 1) * rows_out, :].astype(jnp.bfloat16)
        send_all("mp", lambda j: dn_send.at[j], dn_recv, d_s, d_r)
        dn_recv[mpi] = dn_send[mpi]
        settle(others(sq_all, n), s_s)
        for _ in range(1, mp_halves):
            settle(pr_own, h_s)
        settle(pr_pair, l_s)
        settle(gx_send, gx_s)
        settle(act_all.at[pl.ds(0, owner_halves)], cx_s)
        if owners == n:
            settle(others(gz_send, owner_halves), gz_s)
            settle(act_all.at[pl.ds(0, halves - 1)], cz_s)
        else:
            owning = hi < owner_halves
            pl.when(owning)(lambda: settle(others(gz_send, owner_halves), gz_s))
            pl.when(owning)(lambda: settle(act_all.at[pl.ds(0, halves - 1)], cz_s))
            pl.when(jnp.logical_not(owning))(lambda: settle(gz_send, gz_s))
        settle(others(dn_recv, mp), d_r)
        total = dn_recv[0].astype(jnp.float32)
        for k in range(1, mp):
            total = total + dn_recv[k].astype(jnp.float32)
        own = stream[pl.ds(pl.multiple_of(mpi * rows_out, rows_out), rows_out), :]
        out_ref[...] = (own + total).astype(jnp.bfloat16)

    with scope("drain"):
        settle(others(dn_recv, mp), d_s)


def on_device(
    n, mp,
    queries, root_keys, root_values, mid_keys, mid_values, leaf_keys, leaf_values,
    mid_length, leaf_length, branch_mid, residual, norm_gain,
    out_weight, gate_weight, up_weight, down_weight,
):
    owned, local_heads, hd = queries.shape
    heads = root_keys.shape[1]
    size = local_heads // heads
    own_rows = owned * size
    branches = owned * n
    width = residual.shape[1]
    hidden = gate_weight.shape[1]
    lane_tiles = hidden // 128
    owners = max(k for k in range(2, n + 1, 2) if lane_tiles % k == 0)
    chunk = hidden // owners
    subs, off = [], 0
    for left in range(PIECES, 0, -1):
        count = -(-(chunk - off) // (128 * left)) * 128
        if count:
            subs.append((off, count))
        off += count
    mid_slots = mid_keys.shape[1]
    leaf_slots = leaf_keys.shape[1]
    local_mids = mid_keys.shape[0]
    halves, owner_halves, mp_halves = n // 2, owners // 2, mp // 2
    group = max(1, min(n, ROWS // own_rows))
    pack = min(group, 128 // own_rows)
    tile = math.gcd(width, 256)
    tiles = width // tile

    order = np.zeros((branches * size, branches * size), np.float32)
    at = np.arange(branches * size)
    order[(at % size) * branches + at // size, at] = 1.0

    flat = [
        a.reshape(-1, hd)
        for a in (root_keys, root_values, mid_keys, mid_values, leaf_keys, leaf_values)
    ]
    kv_rows = flat[0].shape[0] + flat[2].shape[0] + flat[4].shape[0]
    span = heads * hd
    bf, f32 = jnp.bfloat16, jnp.float32
    dma = pltpu.SemaphoreType.DMA
    vmem = pl.BlockSpec(memory_space=pltpu.VMEM)
    hbm = pl.BlockSpec(memory_space=pl.ANY)
    rows_out = branches // mp
    scratch = [
        pltpu.SMEM(branch_mid.shape[:1], jnp.int32),
        pltpu.SMEM(mid_length.shape, jnp.int32),
        pltpu.SMEM(leaf_length.shape, jnp.int32),
        pltpu.VMEM((owned, local_heads, hd), bf),
        pltpu.VMEM(order.shape, bf),
        pltpu.VMEM((branches, width), bf),
        pltpu.VMEM((1, width), f32),
        pltpu.VMEM((kv_rows, span), bf),
        pltpu.VMEM((kv_rows, span), bf),
        pltpu.VMEM(out_weight.shape, bf),
        pltpu.VMEM(gate_weight.shape, bf),
        pltpu.VMEM(up_weight.shape, bf),
        pltpu.VMEM(down_weight.shape, bf),
        pltpu.VMEM((own_rows, span), bf),
        pltpu.VMEM((n, own_rows, span), bf),
        pltpu.VMEM((n, own_rows, span), bf),
        pltpu.VMEM((n, own_rows, span), bf),
        pltpu.VMEM((n // pack, 8, 128), f32),
        pltpu.VMEM((n, 8, 128), f32),
        pltpu.VMEM((own_rows, span), f32),
        pltpu.VMEM((128, 128), f32),
        pltpu.VMEM((own_rows, span), bf),
        pltpu.VMEM((n, own_rows, span), bf),
        pltpu.VMEM((branches, local_heads * hd), bf),
        pltpu.VMEM((tiles, branches, tile), bf),
        pltpu.VMEM((mp_halves, tiles, branches, tile), bf),
        pltpu.VMEM((tiles, branches, tile), bf),
        pltpu.VMEM((tiles, branches, tile), bf),
        pltpu.VMEM((branches, width), f32),
        pltpu.VMEM((8, 128), f32),
        pltpu.VMEM((n, 8, 128), f32),
        pltpu.VMEM((128, 128), f32),
        pltpu.VMEM((branches, width), bf),
        pltpu.VMEM((owner_halves, 2, branches, chunk), bf),
        pltpu.VMEM((owner_halves, 2, branches, chunk), bf),
        pltpu.VMEM((2, branches, chunk), f32),
        pltpu.VMEM((owner_halves, 2, branches, chunk), bf),
        pltpu.VMEM((halves, 2, branches, chunk), bf),
        pltpu.VMEM((owners, branches, chunk), bf),
        pltpu.VMEM((branches, width), f32),
        pltpu.VMEM((mp, rows_out, width), bf),
        pltpu.VMEM((mp, rows_out, width), bf),
        dma((7,)),
        dma((2,)),
        dma((4,)),
        dma(()),
        dma((n // group,)),
    ] + [dma(())] * 8 + [
        dma(()),
        dma((mp_halves, tiles)),
        dma(()),
        dma((tiles,)),
        dma(()),
        dma((owner_halves, len(subs))),
        dma(()),
        dma((halves, len(subs))),
        dma(()),
        dma((owner_halves, len(subs))),
        dma(()),
        dma((owner_halves, len(subs))),
        dma(()),
        dma(()),
    ]
    scale2 = hd ** -0.5 * math.log2(math.e)
    return pl.pallas_call(
        functools.partial(
            layer_kernel, n, mp, owners, scale2, local_mids, mid_slots, leaf_slots, size, subs
        ),
        out_shape=pltpu.VMEM((rows_out, width), bf),
        in_specs=[hbm] * 17,
        out_specs=vmem,
        scratch_shapes=scratch,
        compiler_params=pltpu.CompilerParams(
            collective_id=0, has_side_effects=True, vmem_limit_bytes=66900000
        ),
    )(
        branch_mid.reshape(-1), mid_length, leaf_length,
        queries, jnp.asarray(order, bf), residual, norm_gain[None, :],
        *flat, out_weight, gate_weight, up_weight, down_weight,
    )


def solution(mesh):
    in_specs = (
        P("node", "mp", None),
        P("node", "mp", None),
        P("node", "mp", None),
        P("node", None, "mp", None),
        P("node", None, "mp", None),
        P("node", None, "mp", None),
        P("node", None, "mp", None),
        P(),
        P("node"),
        P(),
        P(None, "node"),
        P("node"),
        P("mp", "node"),
        P("node", "mp"),
        P("node", "mp"),
        P("mp", "node"),
    )
    body = functools.partial(on_device, mesh.shape["node"], mesh.shape["mp"])
    return jax.shard_map(
        body, mesh=mesh, in_specs=in_specs, out_specs=P("mp", "node"), check_vma=False
    )
```

```python
import functools
import math
from contextlib import nullcontext as scope

import jax
import jax.numpy as jnp
import numpy as np
from jax import lax
from jax.experimental import pallas as pl
from jax.experimental.pallas import tpu as pltpu
from jax.sharding import PartitionSpec as P

norm_eps = 1e-05
masked_score = -1e30
MESH = pl.DeviceIdType.MESH
ROWS = 256
PIECES = 2


def nt_dot(a, b):
    return lax.dot_general(a, b, (((1,), (1,)), ((), ())), preferred_element_type=jnp.float32)


def nn_dot(a, b):
    return jnp.dot(a, b, preferred_element_type=jnp.float32)


def to_lanes(columns):
    rows = columns[0].shape[0]
    lane = lax.broadcasted_iota(jnp.int32, (rows, 128), 1)
    grid = jnp.zeros((rows, 128), jnp.float32)
    for k, column in enumerate(columns):
        grid = jnp.where(lane == k, column, grid)
    if rows < 128:
        grid = jnp.concatenate([grid] * (128 // rows), axis=0)
    return grid.T


def layer_kernel(
    n, mp, owners, scale2, local_mids, mid_slots, leaf_slots, size, subs,
    mid_of_hbm, mid_len_hbm, leaf_len_hbm, q_hbm, order_hbm, res_hbm, gain_hbm,
    rk_hbm, rv_hbm, mk_hbm, mv_hbm, lk_hbm, lv_hbm, ow_hbm, gw_hbm, uw_hbm, dw_hbm,
    out_ref,
    mid_of, mid_len, leaf_len, q_raw, order_ref, res_ref, gain_ref, keys, values, ow, gw, uw, dw,
    q_own, qall, part_send, part_recv, st_send, st_recv, leaf_part, fac, att_own, att_all, lhs,
    pr_own, pr_hi, pr_pair, pr_lo, stream, sq_own, sq_all, sq_own_scale, xg,
    gx_send, gx_recv, own_sum, gz_send, gz_recv, act_all, acc, dn_send, dn_recv,
    in_sem, kv_sem, w_sem, q_s, q_r, p_s, p_r, t_s, t_r, a_s, a_r, s_s, s_r,
    h_s, h_r, l_s, l_r, gx_s, gx_r, gz_s, gz_r, cz_s, cz_r, cx_s, cx_r, d_s, d_r,
):
    me = lax.axis_index("node")
    mpi = lax.axis_index("mp")
    owned, local_heads, hd = q_raw.shape
    heads = local_heads // size
    own_rows = owned * size
    span = heads * hd
    chunk = act_all.shape[2]
    branches, width = stream.shape
    root = rk_hbm.shape[0]
    mids = mk_hbm.shape[0]
    shared = root + mids
    lo, hi = lax.rem(me, 2), me // 2
    partner = me + 1 - 2 * lo
    halves = n // 2
    owner_halves = owners // 2
    mp_lo, mp_hi = lax.rem(mpi, 2), mpi // 2
    mp_partner = mpi + 1 - 2 * mp_lo
    mp_halves = mp // 2

    in_copies = [
        pltpu.make_async_copy(src, dst, in_sem.at[k])
        for k, (src, dst) in enumerate(
            (
                (q_hbm, q_raw), (order_hbm, order_ref), (res_hbm, res_ref), (gain_hbm, gain_ref),
                (mid_of_hbm, mid_of), (mid_len_hbm, mid_len), (leaf_len_hbm, leaf_len),
            )
        )
    ]
    in_copies[0].start()
    barrier = pltpu.get_barrier_semaphore()

    def greet(axis, here, count):
        def body(i, carry):
            pl.semaphore_signal(
                barrier, inc=1, device_id={axis: lax.rem(here + i, count)}, device_id_type=MESH
            )
            return carry

        lax.fori_loop(1, count, body, 0)

    greet("node", me, n)
    greet("mp", mpi, mp)
    for side, (dst, parts) in enumerate(
        ((keys, (rk_hbm, mk_hbm, lk_hbm)), (values, (rv_hbm, mv_hbm, lv_hbm)))
    ):
        start = 0
        for src in parts:
            rows = src.shape[0]
            pltpu.make_async_copy(
                src, dst.at[pl.ds(start, rows), pl.ds(0, hd)], kv_sem.at[side]
            ).start()
            start += rows
    for copy in in_copies[1:]:
        copy.start()
    w_copies = [
        pltpu.make_async_copy(src, dst, w_sem.at[k])
        for k, (src, dst) in enumerate(((ow_hbm, ow), (gw_hbm, gw), (uw_hbm, uw), (dw_hbm, dw)))
    ]

    def remote(src, dst, send, recv, axis, peer):
        return pltpu.make_async_remote_copy(
            src_ref=src, dst_ref=dst, send_sem=send, recv_sem=recv,
            device_id={axis: peer}, device_id_type=MESH,
        )

    def peers(axis, fn):
        here, count = (me, n) if axis == "node" else (mpi, mp)

        def body(i, carry):
            fn(lax.rem(here + i, count))
            return carry

        lax.fori_loop(1, count, body, 0)

    def send_all(axis, src, dst, send, recv):
        here = me if axis == "node" else mpi
        peers(axis, lambda j: remote(src(j), dst.at[here], send, recv, axis, j).start())

    def settle(ref, sem):
        pltpu.make_async_copy(ref, ref, sem).wait()

    def others(ref, count):
        return ref.at[pl.ds(0, count - 1)]

    with scope("qprep"):
        in_copies[0].wait()
        raw_q = q_raw[...].astype(jnp.float32)
        for h in range(heads):
            q_own[:, h * hd:(h + 1) * hd] = (
                raw_q[:, h * size:(h + 1) * size, :].reshape(own_rows, hd).astype(jnp.bfloat16)
            )
        qall[me] = q_own[...]

    with scope("barrier"):
        pl.semaphore_wait(barrier, n - 1 + mp - 1)
    group = max(1, min(n, ROWS // own_rows))
    groups = n // group

    def send_query(j):
        remote(q_own, qall.at[me], q_s, q_r.at[me // group], "node", j).start()

    def send_near(k, carry):
        send_query(me // group * group + lax.rem(me + k, group))
        return carry

    def send_far(k, carry):
        send_query(lax.rem(me // group * group + k, n))
        return carry

    lax.fori_loop(1, group, send_near, 0)
    lax.fori_loop(group, n, send_far, 0)

    with scope("kvwait"):
        for copy in in_copies[4:]:
            copy.wait()
        for side, ref in enumerate((keys, values)):
            arrived = ref.at[:, pl.ds(0, hd)]
            pltpu.make_async_copy(arrived, arrived, kv_sem.at[side]).wait()
    for copy in w_copies:
        copy.start()

    block = math.gcd(512, math.gcd(shared, leaf_slots * heads))
    row = lax.broadcasted_iota(jnp.int32, (block, hd), 0)
    keep = [(lax.rem(row, heads) == h).astype(jnp.float32).astype(jnp.bfloat16) for h in range(heads)]

    def spread(i, carry):
        at = pl.ds(pl.multiple_of(i * block, block), block)
        for ref in (keys, values):
            mixed = ref[at, 0:hd]
            for h in range(heads):
                ref[at, h * hd:(h + 1) * hd] = mixed * keep[h]
        return carry

    with scope("spread"):
        lax.fori_loop(0, shared // block, spread, 0)

    def attend_rows(query, spans, seen):
        rows = query.shape[0]
        lane = lax.broadcasted_iota(jnp.int32, (rows, 128), 1)
        mine = [lax.rem(lane, heads) == h for h in range(heads)]

        def mix(columns):
            mixed = jnp.broadcast_to(columns[0], lane.shape)
            for h in range(1, heads):
                mixed = jnp.where(mine[h], columns[h], mixed)
            return mixed

        peaks, total, weighted = None, None, None
        for start, count in spans:
            scores = nt_dot(query, keys[start:start + count, :])
            parts = [
                seen(start + k, scores[:, k:k + 128], lane) for k in range(0, count, 128)
            ]
            top = functools.reduce(jnp.maximum, parts)
            now = [
                jnp.max(jnp.where(mine[h], top, -jnp.inf), axis=1, keepdims=True) for h in range(heads)
            ]
            if peaks is not None:
                now = [jnp.maximum(a, b) for a, b in zip(peaks, now)]
                shrink = [jnp.exp2((a - b) * scale2) for a, b in zip(peaks, now)]
                total = total * mix(shrink)
                weighted = weighted * jnp.concatenate(
                    [jnp.broadcast_to(a, (rows, hd)) for a in shrink], axis=1
                )
            peaks = now
            mixed = mix(peaks)
            rounded = []
            for part in parts:
                part = jnp.exp2((part - mixed) * scale2)
                total = part if total is None else total + part
                rounded.append(part.astype(jnp.bfloat16))
            product = nn_dot(jnp.concatenate(rounded, axis=1), values[start:start + count, :])
            weighted = product if weighted is None else weighted + product
        totals = [
            jnp.sum(jnp.where(mine[h], total, 0.0), axis=1, keepdims=True) for h in range(heads)
        ]
        return peaks, totals, weighted

    pack = min(group, 128 // own_rows)
    blocks = group // pack
    rows = group * own_rows
    group_branches = group * owned
    piece = math.gcd(2048, math.gcd(root, mids))

    def attend(i, carry):
        g = lax.rem(me // group + i, groups)

        def each(fn):
            for k in range(group):
                j = g * group + lax.rem(me - g * group + group // 2 + k + group, group)
                pl.when(j != me)(functools.partial(fn, j))

        pl.when(g == me // group)(lambda: settle(qall.at[pl.ds(0, group - 1)], q_r.at[g]))
        if groups > 1:
            pl.when(g != me // group)(lambda: settle(qall.at[pl.ds(0, group)], q_r.at[g]))
        lows, highs = [], []
        for b in range(group_branches):
            mid = mid_of[g * group_branches + b]
            local = mid - me * local_mids
            here = (local >= 0) & (local < local_mids)
            low = local * (mid_slots * heads)
            highs.append(jnp.full((size, 128), jnp.where(here, low + mid_len[mid] * heads, 0), jnp.int32))
            lows.append(jnp.full((size, 128), jnp.where(here, low, 0), jnp.int32))
        low, high = jnp.concatenate(lows, axis=0), jnp.concatenate(highs, axis=0)
        query = qall[pl.ds(g * group, group)].reshape(rows, span)

        def seen(start, part, lane):
            if start < root:
                return part
            column = lane + (start - root)
            kept = column < high
            if local_mids > 1:
                kept = kept & (column >= low)
            return jnp.where(kept, part, masked_score)

        tops, totals, weighted = attend_rows(
            query, [(start, piece) for start in range(0, shared, piece)], seen
        )
        part_send[pl.ds(g * group, group)] = weighted.astype(jnp.bfloat16).reshape(group, own_rows, span)
        columns = tops + totals
        for k in range(blocks):
            at = slice(k * pack * own_rows, (k + 1) * pack * own_rows)
            st_send[g * blocks + k] = to_lanes([column[at] for column in columns])[0:8]

        def send(j):
            remote(part_send.at[j], part_recv.at[me], p_s, p_r, "node", j).start()
            remote(st_send.at[j // pack], st_recv.at[me], t_s, t_r, "node", j).start()

        each(send)
        return carry

    with scope("attend"):
        lax.fori_loop(0, groups, attend, 0)
    part_recv[me] = part_send[me]
    st_recv[me] = st_send[me // pack]

    with scope("leaf"):
        lax.fori_loop(shared // block, keys.shape[0] // block, spread, 0)
        leaf_rows = leaf_slots * heads
        stats = []
        for b in range(owned):
            start = shared + b * leaf_rows
            tops, totals, weighted = attend_rows(
                q_own[b * size:(b + 1) * size, :],
                [(start, leaf_rows)],
                lambda at, part, lane: jnp.where(
                    lane + (at - start) < leaf_len[b] * heads, part, masked_score
                ),
            )
            leaf_part[b * size:(b + 1) * size, :] = weighted
            stats.append(tops + totals)
        leaf_stats = to_lanes([
            jnp.concatenate([stats[b][k] for b in range(owned)], axis=0) for k in range(2 * heads)
        ])[0:8]

    with scope("partx"):
        settle(others(part_recv, n), p_r)
        settle(others(st_recv, n), t_r)

    with scope("merge"):
        factors = []
        leaf_factors = []
        for h in range(heads):
            peak = jnp.concatenate([st_recv[i, h:h + 1, :] for i in range(n)], axis=0)
            total = jnp.concatenate([st_recv[i, heads + h:heads + h + 1, :] for i in range(n)], axis=0)
            leaf_peak, leaf_total = leaf_stats[h:h + 1], leaf_stats[heads + h:heads + h + 1]
            top = jnp.maximum(jnp.max(peak, axis=0, keepdims=True), leaf_peak)
            scale, leaf_scale = jnp.exp2((peak - top) * scale2), jnp.exp2((leaf_peak - top) * scale2)
            whole = jnp.sum(total * scale, axis=0, keepdims=True) + leaf_total * leaf_scale
            factors.append(scale / whole)
            leaf_factors.append(leaf_scale / whole)
        used = heads * n + heads
        table = jnp.concatenate(
            factors + leaf_factors + [jnp.zeros((128 - used, 128), jnp.float32)], axis=0
        )
        fac[...] = table.T
        mine = fac[pl.ds(pl.multiple_of(lax.rem(me, pack) * own_rows, own_rows), own_rows), :]
        for h in range(heads):
            at = slice(h * hd, (h + 1) * hd)
            sum_h = leaf_part[:, at] * mine[:, heads * n + h:heads * n + h + 1]
            for i in range(n):
                sum_h = sum_h + part_recv[i, :, at].astype(jnp.float32) * mine[:, h * n + i:h * n + i + 1]
            att_own[:, at] = sum_h.astype(jnp.bfloat16)

    with scope("attag"):
        send_all("node", lambda j: att_own, att_all, a_s, a_r)
        att_all[me] = att_own[...]
        in_copies[1].wait()
        settle(others(att_all, n), a_r)

    with scope("order"):
        mixed = nn_dot(order_ref[...], att_all[...].reshape(n * own_rows, span)).astype(jnp.bfloat16)
        for h in range(heads):
            for g in range(size):
                first = (h * size + g) * hd
                lhs[:, first:first + hd] = mixed[g * branches:(g + 1) * branches, h * hd:(h + 1) * hd]

    w_copies[0].wait()
    tiles, tile = pr_own.shape[0], pr_own.shape[2]

    def mp_peer(k):
        return lax.rem(mp_hi + k, mp_halves) * 2 + mp_lo

    def project(t, carry):
        at = pl.ds(pl.multiple_of(t * tile, tile), tile)
        value = nn_dot(lhs[...], ow[:, at])
        stream[:, at] = value
        pr_own[t] = value.astype(jnp.bfloat16)
        for k in range(1, mp_halves):
            peer = mp_peer(k)
            remote(
                pr_own.at[t], pr_hi.at[mp_hi, t], h_s, h_r.at[mp_hi, t], "mp", peer
            ).start()
        return carry

    def pair(t, carry):
        at = pl.ds(pl.multiple_of(t * tile, tile), tile)
        value = stream[:, at]
        for k in range(1, mp_halves):
            peer = mp_peer(k)
            at_hi = peer // 2
            remote(
                pr_own.at[t], pr_hi.at[at_hi, t], h_s, h_r.at[at_hi, t], "mp", peer
            ).wait_recv()
            value = value + pr_hi[at_hi, t].astype(jnp.float32)
        stream[:, at] = value
        pr_pair[t] = value.astype(jnp.bfloat16)
        remote(pr_pair.at[t], pr_lo.at[t], l_s, l_r.at[t], "mp", mp_partner).start()
        return carry

    def finish(t, squares):
        at = pl.ds(pl.multiple_of(t * tile, tile), tile)
        remote(pr_pair.at[t], pr_lo.at[t], l_s, l_r.at[t], "mp", mp_partner).wait_recv()
        value = stream[:, at] + pr_lo[t].astype(jnp.float32) + res_ref[:, at].astype(jnp.float32)
        stream[:, at] = value
        xg[:, at] = (value * gain_ref[:, at]).astype(jnp.bfloat16)
        return squares + jnp.sum(value * value, axis=1, keepdims=True)

    with scope("project"):
        lax.fori_loop(0, tiles, project, 0)
    with scope("prhi"):
        in_copies[2].wait()
        in_copies[3].wait()
        lax.fori_loop(0, tiles, pair, 0)
    with scope("prlo"):
        squares = lax.fori_loop(0, tiles, finish, jnp.zeros((branches, 1), jnp.float32))

    def early_sent():
        settle(others(qall, n), q_s)
        settle(others(part_recv, n), p_s)
        settle(others(st_recv, n), t_s)
        settle(others(att_all, n), a_s)

    with scope("wwait12"):
        w_copies[1].wait()
        w_copies[2].wait()

    def turn(i):
        down = jnp.where(owner_halves - 1 - i > hi, owner_halves - 1 - i, owner_halves - 2 - i)
        up = jnp.where(i < hi, i, i + 1)
        other = jnp.where(2 * hi >= owner_halves, up, down)
        return jnp.where((i == owner_halves - 1) & (hi < owner_halves), hi, other)

    def gate_up(j, off, count):
        at = pl.ds(pl.multiple_of(j * chunk + off, 128), count)
        return nn_dot(xg[...], gw[:, at]), nn_dot(xg[...], uw[:, at])

    def gx(k, s):
        at = pl.ds(subs[s][0], subs[s][1])
        return remote(
            gx_send.at[k, :, :, at], gx_recv.at[k, :, :, at], gx_s, gx_r.at[k, s], "node", partner
        )

    def gz(k, target, slot, s):
        at = pl.ds(subs[s][0], subs[s][1])
        return remote(
            gz_send.at[k, :, :, at], gz_recv.at[slot, :, :, at], gz_s, gz_r.at[slot, s],
            "node", target * 2 + lo,
        )

    line = halves == 4 and owner_halves == 4
    outer = (hi == 0) | (hi == 3)
    beside = hi + 1 - 2 * lax.rem(hi, 2)
    across_outer = jnp.where(hi < 2, 3, 0)
    across_inner = jnp.where(hi < 2, 2, 1)
    line_turn = (
        jnp.where(outer, across_outer, beside),
        jnp.where(outer, across_inner, across_outer),
        jnp.where(outer, beside, across_inner),
        hi,
    )

    def partner_side(s, k):
        off, count = subs[s]
        gate, upward = gate_up(k * 2 + 1 - lo, off, count)
        gx_send[k, 0, :, off:off + count] = gate.astype(jnp.bfloat16)
        gx_send[k, 1, :, off:off + count] = upward.astype(jnp.bfloat16)
        gx(k, s).start()

    def own_side(s, k):
        off, count = subs[s]
        at = slice(off, off + count)
        gate, upward = gate_up(k * 2 + lo, off, count)
        gx(k, s).wait_recv()
        gate = gate + gx_recv[k, 0, :, at].astype(jnp.float32)
        upward = upward + gx_recv[k, 1, :, at].astype(jnp.float32)
        return gate, upward

    def keep_own(s, gate, upward):
        at = slice(subs[s][0], subs[s][0] + subs[s][1])
        own_sum[0, :, at] = gate
        own_sum[1, :, at] = upward

    def pass_on(s, k, target, slot, gate, upward):
        at = slice(subs[s][0], subs[s][0] + subs[s][1])
        gz_send[k, 0, :, at] = gate.astype(jnp.bfloat16)
        gz_send[k, 1, :, at] = upward.astype(jnp.bfloat16)
        gz(k, target, slot, s).start()

    def own_line(s, p):
        at = slice(subs[s][0], subs[s][0] + subs[s][1])
        k = line_turn[p]
        gate, upward = own_side(s, k)
        if p == 3:
            keep_own(s, gate, upward)
        elif p == 0:
            pass_on(s, k, beside, jnp.where(outer, 0, 2), gate, upward)
        else:
            held = p - 1

            @pl.when(outer)
            def _():
                pass_on(s, k, beside, p, gate, upward)

            @pl.when(jnp.logical_not(outer))
            def _():
                gz(k, beside, held, s).wait_recv()
                pass_on(
                    s, k, k, 3,
                    gate + gz_recv[held, 0, :, at].astype(jnp.float32),
                    upward + gz_recv[held, 1, :, at].astype(jnp.float32),
                )

    def own_direct(s, k):
        gate, upward = own_side(s, k)
        pl.when(k == hi)(lambda: keep_own(s, gate, upward))
        pl.when(k != hi)(lambda: pass_on(s, k, k, hi, gate, upward))

    def partner_turns(i, carry):
        for s in range(len(subs)):
            partner_side(s, turn(i))
        return carry

    def own_turns(i, carry):
        for s in range(len(subs)):
            own_direct(s, turn(i))
        return carry

    def act_z(k, s, owner, sem_at):
        at = pl.ds(subs[s][0], subs[s][1])
        return remote(
            act_all.at[owner, :, at], act_all.at[owner, :, at], cz_s, cz_r.at[sem_at, s],
            "node", k * 2 + lo,
        )

    def act_x(k, s, side):
        owner = k * 2 + side
        at = pl.ds(subs[s][0], subs[s][1])
        return remote(
            act_all.at[owner, :, at], act_all.at[owner, :, at], cx_s, cx_r.at[k, s], "node", partner
        )

    def other_halves(fn):
        def body(i, carry):
            down = jnp.where(halves - 1 - i > hi, halves - 1 - i, halves - 2 - i)
            fn(jnp.where(2 * hi >= halves, jnp.where(i < hi, i, i + 1), down))
            return carry

        lax.fori_loop(0, halves - 1, lambda i, carry: body(halves - 2 - i, carry), 0)

    def norm_scale():
        settle(others(sq_all, n), s_r)
        total = sq_all[0]
        for k in range(1, n):
            total = total + sq_all[k]
        mean = total / (width * n)
        sq_own_scale[...] = jnp.concatenate([lax.rsqrt(mean + norm_eps)] * 16, axis=0).T

    def owner_work(s):
        off, count = subs[s]
        at = slice(off, off + count)
        root_mean = sq_own_scale[0:branches, 0:1]

        def add(k, carry):
            return (
                carry[0] + gz_recv[k, 0, :, at].astype(jnp.float32),
                carry[1] + gz_recv[k, 1, :, at].astype(jnp.float32),
            )

        gate, upward = own_sum[0, :, at], own_sum[1, :, at]
        if line:
            for slot in (2, 3):
                gz(0, beside, slot, s).wait_recv()
                gate, upward = add(slot, (gate, upward))
        else:
            other_halves(lambda k: gz(0, k, k, s).wait_recv())
            gate, upward = lax.fori_loop(
                1, halves, lambda i, carry: add(lax.rem(hi + i, halves), carry), (gate, upward)
            )
        gate, upward = gate * root_mean, upward * root_mean
        act_all[me, :, at] = (gate / (1.0 + jnp.exp(-gate)) * upward).astype(jnp.bfloat16)
        act_x(hi, s, lo).start()
        other_halves(lambda k: act_z(k, s, me, hi).start())

    def own_act(s):
        if owners == n:
            owner_work(s)
        else:
            pl.when(me < owners)(functools.partial(owner_work, s))

    def down(owner, s):
        off, count = subs[s]
        at = pl.ds(pl.multiple_of(owner * chunk + off, 128), count)
        acc[...] += nn_dot(act_all[owner, :, off:off + count], dw[at, :])

    def forward_turns(i, carry):
        k = turn(owner_halves - 1 - i)
        for s in range(steps):
            @pl.when(k != hi)
            def _():
                act_z(k, s, k * 2 + lo, k).wait_recv()
                act_x(k, s, lo).start()

        for s in range(steps):
            down(k * 2 + lo, s)
        return carry

    def partner_acts(i, carry):
        k = turn(owner_halves - 1 - i)
        for s in range(steps):
            act_x(k, s, 1 - lo).wait_recv()
            down(k * 2 + 1 - lo, s)
        return carry

    steps = len(subs)
    acc[...] = jnp.zeros(acc.shape, jnp.float32)
    with scope("gupartner"):
        if line:
            for p in range(4):
                for s in range(steps):
                    partner_side(s, line_turn[p])
        else:
            lax.fori_loop(0, owner_halves, partner_turns, 0)
    with scope("sqsend"):
        sq_own[...] = to_lanes([squares])[0:8]
        send_all("node", lambda j: sq_own, sq_all, s_s, s_r)
        sq_all[me] = sq_own[...]
        early_sent()
    if line:
        for p in range(4):
            if p == 3:
                norm_scale()
            for s in range(steps):
                with scope(f"own{p}{s}"):
                    own_line(s, p)
    else:
        lax.fori_loop(0, owner_halves, own_turns, 0)
        norm_scale()
    w_copies[3].wait()
    for s in range(steps):
        with scope(f"act{s}"):
            own_act(s)
    with scope("forward"):
        lax.fori_loop(0, owner_halves, forward_turns, 0)
    with scope("frompartner"):
        lax.fori_loop(0, owner_halves, partner_acts, 0)

    rows_out = out_ref.shape[0]
    with scope("dnx"):
        for k in range(mp):
            dn_send[k] = acc[k * rows_out:(k + 1) * rows_out, :].astype(jnp.bfloat16)
        send_all("mp", lambda j: dn_send.at[j], dn_recv, d_s, d_r)
        dn_recv[mpi] = dn_send[mpi]
        settle(others(sq_all, n), s_s)
        for _ in range(1, mp_halves):
            settle(pr_own, h_s)
        settle(pr_pair, l_s)
        settle(gx_send, gx_s)
        settle(act_all.at[pl.ds(0, owner_halves)], cx_s)
        if owners == n:
            settle(others(gz_send, owner_halves), gz_s)
            settle(act_all.at[pl.ds(0, halves - 1)], cz_s)
        else:
            owning = hi < owner_halves
            pl.when(owning)(lambda: settle(others(gz_send, owner_halves), gz_s))
            pl.when(owning)(lambda: settle(act_all.at[pl.ds(0, halves - 1)], cz_s))
            pl.when(jnp.logical_not(owning))(lambda: settle(gz_send, gz_s))
        settle(others(dn_recv, mp), d_r)
        total = dn_recv[0].astype(jnp.float32)
        for k in range(1, mp):
            total = total + dn_recv[k].astype(jnp.float32)
        own = stream[pl.ds(pl.multiple_of(mpi * rows_out, rows_out), rows_out), :]
        out_ref[...] = (own + total).astype(jnp.bfloat16)

    with scope("drain"):
        settle(others(dn_recv, mp), d_s)


def on_device(
    n, mp,
    queries, root_keys, root_values, mid_keys, mid_values, leaf_keys, leaf_values,
    mid_length, leaf_length, branch_mid, residual, norm_gain,
    out_weight, gate_weight, up_weight, down_weight,
):
    owned, local_heads, hd = queries.shape
    heads = root_keys.shape[1]
    size = local_heads // heads
    own_rows = owned * size
    branches = owned * n
    width = residual.shape[1]
    hidden = gate_weight.shape[1]
    lane_tiles = hidden // 128
    owners = max(k for k in range(2, n + 1, 2) if lane_tiles % k == 0)
    chunk = hidden // owners
    subs, off = [], 0
    for left in range(PIECES, 0, -1):
        count = -(-(chunk - off) // (128 * left)) * 128
        if count:
            subs.append((off, count))
        off += count
    mid_slots = mid_keys.shape[1]
    leaf_slots = leaf_keys.shape[1]
    local_mids = mid_keys.shape[0]
    halves, owner_halves, mp_halves = n // 2, owners // 2, mp // 2
    group = max(1, min(n, ROWS // own_rows))
    pack = min(group, 128 // own_rows)
    tile = math.gcd(width, 256)
    tiles = width // tile

    order = np.zeros((branches * size, branches * size), np.float32)
    at = np.arange(branches * size)
    order[(at % size) * branches + at // size, at] = 1.0

    flat = [
        a.reshape(-1, hd)
        for a in (root_keys, root_values, mid_keys, mid_values, leaf_keys, leaf_values)
    ]
    kv_rows = flat[0].shape[0] + flat[2].shape[0] + flat[4].shape[0]
    span = heads * hd
    bf, f32 = jnp.bfloat16, jnp.float32
    dma = pltpu.SemaphoreType.DMA
    vmem = pl.BlockSpec(memory_space=pltpu.VMEM)
    hbm = pl.BlockSpec(memory_space=pl.ANY)
    rows_out = branches // mp
    scratch = [
        pltpu.SMEM(branch_mid.shape[:1], jnp.int32),
        pltpu.SMEM(mid_length.shape, jnp.int32),
        pltpu.SMEM(leaf_length.shape, jnp.int32),
        pltpu.VMEM((owned, local_heads, hd), bf),
        pltpu.VMEM(order.shape, bf),
        pltpu.VMEM((branches, width), bf),
        pltpu.VMEM((1, width), f32),
        pltpu.VMEM((kv_rows, span), bf),
        pltpu.VMEM((kv_rows, span), bf),
        pltpu.VMEM(out_weight.shape, bf),
        pltpu.VMEM(gate_weight.shape, bf),
        pltpu.VMEM(up_weight.shape, bf),
        pltpu.VMEM(down_weight.shape, bf),
        pltpu.VMEM((own_rows, span), bf),
        pltpu.VMEM((n, own_rows, span), bf),
        pltpu.VMEM((n, own_rows, span), bf),
        pltpu.VMEM((n, own_rows, span), bf),
        pltpu.VMEM((n // pack, 8, 128), f32),
        pltpu.VMEM((n, 8, 128), f32),
        pltpu.VMEM((own_rows, span), f32),
        pltpu.VMEM((128, 128), f32),
        pltpu.VMEM((own_rows, span), bf),
        pltpu.VMEM((n, own_rows, span), bf),
        pltpu.VMEM((branches, local_heads * hd), bf),
        pltpu.VMEM((tiles, branches, tile), bf),
        pltpu.VMEM((mp_halves, tiles, branches, tile), bf),
        pltpu.VMEM((tiles, branches, tile), bf),
        pltpu.VMEM((tiles, branches, tile), bf),
        pltpu.VMEM((branches, width), f32),
        pltpu.VMEM((8, 128), f32),
        pltpu.VMEM((n, 8, 128), f32),
        pltpu.VMEM((128, 128), f32),
        pltpu.VMEM((branches, width), bf),
        pltpu.VMEM((owner_halves, 2, branches, chunk), bf),
        pltpu.VMEM((owner_halves, 2, branches, chunk), bf),
        pltpu.VMEM((2, branches, chunk), f32),
        pltpu.VMEM((owner_halves, 2, branches, chunk), bf),
        pltpu.VMEM((halves, 2, branches, chunk), bf),
        pltpu.VMEM((owners, branches, chunk), bf),
        pltpu.VMEM((branches, width), f32),
        pltpu.VMEM((mp, rows_out, width), bf),
        pltpu.VMEM((mp, rows_out, width), bf),
        dma((7,)),
        dma((2,)),
        dma((4,)),
        dma(()),
        dma((n // group,)),
    ] + [dma(())] * 8 + [
        dma(()),
        dma((mp_halves, tiles)),
        dma(()),
        dma((tiles,)),
        dma(()),
        dma((owner_halves, len(subs))),
        dma(()),
        dma((halves, len(subs))),
        dma(()),
        dma((owner_halves, len(subs))),
        dma(()),
        dma((owner_halves, len(subs))),
        dma(()),
        dma(()),
    ]
    scale2 = hd ** -0.5 * math.log2(math.e)
    return pl.pallas_call(
        functools.partial(
            layer_kernel, n, mp, owners, scale2, local_mids, mid_slots, leaf_slots, size, subs
        ),
        out_shape=pltpu.VMEM((rows_out, width), bf),
        in_specs=[hbm] * 17,
        out_specs=vmem,
        scratch_shapes=scratch,
        compiler_params=pltpu.CompilerParams(
            collective_id=0, has_side_effects=True, vmem_limit_bytes=66900000
        ),
    )(
        branch_mid.reshape(-1), mid_length, leaf_length,
        queries, jnp.asarray(order, bf), residual, norm_gain[None, :],
        *flat, out_weight, gate_weight, up_weight, down_weight,
    )


def solution(mesh):
    in_specs = (
        P("node", "mp", None),
        P("node", "mp", None),
        P("node", "mp", None),
        P("node", None, "mp", None),
        P("node", None, "mp", None),
        P("node", None, "mp", None),
        P("node", None, "mp", None),
        P(),
        P("node"),
        P(),
        P(None, "node"),
        P("node"),
        P("mp", "node"),
        P("node", "mp"),
        P("node", "mp"),
        P("mp", "node"),
    )
    body = functools.partial(on_device, mesh.shape["node"], mesh.shape["mp"])
    return jax.shard_map(
        body, mesh=mesh, in_specs=in_specs, out_specs=P("mp", "node"), check_vma=False
    )
```

```python
import functools
import math
from contextlib import nullcontext as scope

import jax
import jax.numpy as jnp
import numpy as np
from jax import lax
from jax.experimental import pallas as pl
from jax.experimental.pallas import tpu as pltpu
from jax.sharding import PartitionSpec as P

norm_eps = 1e-05
masked_score = -1e30
MESH = pl.DeviceIdType.MESH
ROWS = 256
PIECES = 2


def nt_dot(a, b):
    return lax.dot_general(a, b, (((1,), (1,)), ((), ())), preferred_element_type=jnp.float32)


def nn_dot(a, b):
    return jnp.dot(a, b, preferred_element_type=jnp.float32)


def to_lanes(columns):
    rows = columns[0].shape[0]
    lane = lax.broadcasted_iota(jnp.int32, (rows, 128), 1)
    grid = jnp.zeros((rows, 128), jnp.float32)
    for k, column in enumerate(columns):
        grid = jnp.where(lane == k, column, grid)
    if rows < 128:
        grid = jnp.concatenate([grid] * (128 // rows), axis=0)
    return grid.T


def layer_kernel(
    n, mp, owners, scale2, local_mids, mid_slots, leaf_slots, size, subs,
    mid_of_hbm, mid_len_hbm, leaf_len_hbm, q_hbm, order_hbm, res_hbm, gain_hbm,
    rk_hbm, rv_hbm, mk_hbm, mv_hbm, lk_hbm, lv_hbm, ow_hbm, gw_hbm, uw_hbm, dw_hbm,
    out_ref,
    mid_of, mid_len, leaf_len, q_raw, order_ref, res_ref, gain_ref, keys, values, ow, gw, uw, dw,
    q_own, qall, part_send, part_recv, st_send, st_recv, leaf_part, fac, att_own, att_all, lhs,
    pr_own, pr_hi, pr_pair, pr_lo, stream, sq_own, sq_all, sq_own_scale, xg,
    gx_send, gx_recv, own_sum, gz_send, gz_recv, act_all, acc, dn_send, dn_recv,
    in_sem, kv_sem, w_sem, q_s, q_r, p_s, p_r, t_s, t_r, a_s, a_r, s_s, s_r,
    h_s, h_r, l_s, l_r, gx_s, gx_r, gz_s, gz_r, cz_s, cz_r, cx_s, cx_r, d_s, d_r,
):
    me = lax.axis_index("node")
    mpi = lax.axis_index("mp")
    owned, local_heads, hd = q_raw.shape
    heads = local_heads // size
    own_rows = owned * size
    span = heads * hd
    chunk = act_all.shape[2]
    branches, width = stream.shape
    root = rk_hbm.shape[0]
    mids = mk_hbm.shape[0]
    shared = root + mids
    lo, hi = lax.rem(me, 2), me // 2
    partner = me + 1 - 2 * lo
    halves = n // 2
    owner_halves = owners // 2
    mp_lo, mp_hi = lax.rem(mpi, 2), mpi // 2
    mp_partner = mpi + 1 - 2 * mp_lo
    mp_halves = mp // 2

    in_copies = [
        pltpu.make_async_copy(src, dst, in_sem.at[k])
        for k, (src, dst) in enumerate(
            (
                (q_hbm, q_raw), (order_hbm, order_ref), (res_hbm, res_ref), (gain_hbm, gain_ref),
                (mid_of_hbm, mid_of), (mid_len_hbm, mid_len), (leaf_len_hbm, leaf_len),
            )
        )
    ]
    in_copies[0].start()
    barrier = pltpu.get_barrier_semaphore()

    def greet(axis, here, count):
        def body(i, carry):
            pl.semaphore_signal(
                barrier, inc=1, device_id={axis: lax.rem(here + i, count)}, device_id_type=MESH
            )
            return carry

        lax.fori_loop(1, count, body, 0)

    greet("node", me, n)
    greet("mp", mpi, mp)
    for side, (dst, parts) in enumerate(
        ((keys, (rk_hbm, mk_hbm, lk_hbm)), (values, (rv_hbm, mv_hbm, lv_hbm)))
    ):
        start = 0
        for src in parts:
            rows = src.shape[0]
            pltpu.make_async_copy(
                src, dst.at[pl.ds(start, rows), pl.ds(0, hd)], kv_sem.at[side]
            ).start()
            start += rows
    for copy in in_copies[1:]:
        copy.start()
    w_copies = [
        pltpu.make_async_copy(src, dst, w_sem.at[k])
        for k, (src, dst) in enumerate(((ow_hbm, ow), (gw_hbm, gw), (uw_hbm, uw), (dw_hbm, dw)))
    ]

    def remote(src, dst, send, recv, axis, peer):
        return pltpu.make_async_remote_copy(
            src_ref=src, dst_ref=dst, send_sem=send, recv_sem=recv,
            device_id={axis: peer}, device_id_type=MESH,
        )

    def peers(axis, fn):
        here, count = (me, n) if axis == "node" else (mpi, mp)

        def body(i, carry):
            fn(lax.rem(here + i, count))
            return carry

        lax.fori_loop(1, count, body, 0)

    def send_all(axis, src, dst, send, recv):
        here = me if axis == "node" else mpi
        peers(axis, lambda j: remote(src(j), dst.at[here], send, recv, axis, j).start())

    def settle(ref, sem):
        pltpu.make_async_copy(ref, ref, sem).wait()

    def others(ref, count):
        return ref.at[pl.ds(0, count - 1)]

    with scope("qprep"):
        in_copies[0].wait()
        raw_q = q_raw[...].astype(jnp.float32)
        for h in range(heads):
            q_own[:, h * hd:(h + 1) * hd] = (
                raw_q[:, h * size:(h + 1) * size, :].reshape(own_rows, hd).astype(jnp.bfloat16)
            )
        qall[me] = q_own[...]

    with scope("barrier"):
        pl.semaphore_wait(barrier, n - 1 + mp - 1)
    group = max(1, min(n, ROWS // own_rows))
    groups = n // group

    def send_query(j):
        remote(q_own, qall.at[me], q_s, q_r.at[me // group], "node", j).start()

    def send_near(k, carry):
        send_query(me // group * group + lax.rem(me + k, group))
        return carry

    def send_far(k, carry):
        send_query(lax.rem(me // group * group + k, n))
        return carry

    lax.fori_loop(1, group, send_near, 0)
    lax.fori_loop(group, n, send_far, 0)

    with scope("kvwait"):
        for copy in in_copies[4:]:
            copy.wait()
        for side, ref in enumerate((keys, values)):
            arrived = ref.at[:, pl.ds(0, hd)]
            pltpu.make_async_copy(arrived, arrived, kv_sem.at[side]).wait()
    for copy in w_copies:
        copy.start()

    block = math.gcd(512, math.gcd(shared, leaf_slots * heads))
    row = lax.broadcasted_iota(jnp.int32, (block, hd), 0)
    keep = [(lax.rem(row, heads) == h).astype(jnp.float32).astype(jnp.bfloat16) for h in range(heads)]

    def spread(i, carry):
        at = pl.ds(pl.multiple_of(i * block, block), block)
        for ref in (keys, values):
            mixed = ref[at, 0:hd]
            for h in range(heads):
                ref[at, h * hd:(h + 1) * hd] = mixed * keep[h]
        return carry

    with scope("spread"):
        lax.fori_loop(0, shared // block, spread, 0)

    def attend_rows(query, spans, seen):
        rows = query.shape[0]
        lane = lax.broadcasted_iota(jnp.int32, (rows, 128), 1)
        mine = [lax.rem(lane, heads) == h for h in range(heads)]

        def mix(columns):
            mixed = jnp.broadcast_to(columns[0], lane.shape)
            for h in range(1, heads):
                mixed = jnp.where(mine[h], columns[h], mixed)
            return mixed

        peaks, total, weighted = None, None, None
        for start, count in spans:
            scores = nt_dot(query, keys[start:start + count, :])
            parts = [
                seen(start + k, scores[:, k:k + 128], lane) for k in range(0, count, 128)
            ]
            top = functools.reduce(jnp.maximum, parts)
            now = [
                jnp.max(jnp.where(mine[h], top, -jnp.inf), axis=1, keepdims=True) for h in range(heads)
            ]
            if peaks is not None:
                now = [jnp.maximum(a, b) for a, b in zip(peaks, now)]
                shrink = [jnp.exp2((a - b) * scale2) for a, b in zip(peaks, now)]
                total = total * mix(shrink)
                weighted = weighted * jnp.concatenate(
                    [jnp.broadcast_to(a, (rows, hd)) for a in shrink], axis=1
                )
            peaks = now
            mixed = mix(peaks)
            rounded = []
            for part in parts:
                part = jnp.exp2((part - mixed) * scale2)
                total = part if total is None else total + part
                rounded.append(part.astype(jnp.bfloat16))
            product = nn_dot(jnp.concatenate(rounded, axis=1), values[start:start + count, :])
            weighted = product if weighted is None else weighted + product
        totals = [
            jnp.sum(jnp.where(mine[h], total, 0.0), axis=1, keepdims=True) for h in range(heads)
        ]
        return peaks, totals, weighted

    pack = min(group, 128 // own_rows)
    blocks = group // pack
    rows = group * own_rows
    group_branches = group * owned
    piece = math.gcd(2048, math.gcd(root, mids))

    def attend(i, carry):
        g = lax.rem(me // group + i, groups)

        def each(fn):
            for k in range(group):
                j = g * group + lax.rem(me + group // 2 + k, group)
                pl.when(j != me)(functools.partial(fn, j))

        pl.when(g == me // group)(lambda: settle(qall.at[pl.ds(0, group - 1)], q_r.at[g]))
        if groups > 1:
            pl.when(g != me // group)(lambda: settle(qall.at[pl.ds(0, group)], q_r.at[g]))
        lows, highs = [], []
        for b in range(group_branches):
            mid = mid_of[g * group_branches + b]
            local = mid - me * local_mids
            here = (local >= 0) & (local < local_mids)
            low = local * (mid_slots * heads)
            highs.append(jnp.full((size, 128), jnp.where(here, low + mid_len[mid] * heads, 0), jnp.int32))
            lows.append(jnp.full((size, 128), jnp.where(here, low, 0), jnp.int32))
        low, high = jnp.concatenate(lows, axis=0), jnp.concatenate(highs, axis=0)
        query = qall[pl.ds(g * group, group)].reshape(rows, span)

        def seen(start, part, lane):
            if start < root:
                return part
            column = lane + (start - root)
            kept = column < high
            if local_mids > 1:
                kept = kept & (column >= low)
            return jnp.where(kept, part, masked_score)

        tops, totals, weighted = attend_rows(
            query, [(start, piece) for start in range(0, shared, piece)], seen
        )
        part_send[pl.ds(g * group, group)] = weighted.astype(jnp.bfloat16).reshape(group, own_rows, span)
        columns = tops + totals
        for k in range(blocks):
            at = slice(k * pack * own_rows, (k + 1) * pack * own_rows)
            st_send[g * blocks + k] = to_lanes([column[at] for column in columns])[0:8]

        def send(j):
            remote(part_send.at[j], part_recv.at[me], p_s, p_r, "node", j).start()
            remote(st_send.at[j // pack], st_recv.at[me], t_s, t_r, "node", j).start()

        each(send)
        return carry

    with scope("attend"):
        lax.fori_loop(0, groups, attend, 0)
    part_recv[me] = part_send[me]
    st_recv[me] = st_send[me // pack]

    with scope("leaf"):
        lax.fori_loop(shared // block, keys.shape[0] // block, spread, 0)
        leaf_rows = leaf_slots * heads
        stats = []
        for b in range(owned):
            start = shared + b * leaf_rows
            tops, totals, weighted = attend_rows(
                q_own[b * size:(b + 1) * size, :],
                [(start, leaf_rows)],
                lambda at, part, lane: jnp.where(
                    lane + (at - start) < leaf_len[b] * heads, part, masked_score
                ),
            )
            leaf_part[b * size:(b + 1) * size, :] = weighted
            stats.append(tops + totals)
        leaf_stats = to_lanes([
            jnp.concatenate([stats[b][k] for b in range(owned)], axis=0) for k in range(2 * heads)
        ])[0:8]

    with scope("partx"):
        settle(others(part_recv, n), p_r)
        settle(others(st_recv, n), t_r)

    with scope("merge"):
        factors = []
        leaf_factors = []
        for h in range(heads):
            peak = jnp.concatenate([st_recv[i, h:h + 1, :] for i in range(n)], axis=0)
            total = jnp.concatenate([st_recv[i, heads + h:heads + h + 1, :] for i in range(n)], axis=0)
            leaf_peak, leaf_total = leaf_stats[h:h + 1], leaf_stats[heads + h:heads + h + 1]
            top = jnp.maximum(jnp.max(peak, axis=0, keepdims=True), leaf_peak)
            scale, leaf_scale = jnp.exp2((peak - top) * scale2), jnp.exp2((leaf_peak - top) * scale2)
            whole = jnp.sum(total * scale, axis=0, keepdims=True) + leaf_total * leaf_scale
            factors.append(scale / whole)
            leaf_factors.append(leaf_scale / whole)
        used = heads * n + heads
        table = jnp.concatenate(
            factors + leaf_factors + [jnp.zeros((128 - used, 128), jnp.float32)], axis=0
        )
        fac[...] = table.T
        mine = fac[pl.ds(pl.multiple_of(lax.rem(me, pack) * own_rows, own_rows), own_rows), :]
        for h in range(heads):
            at = slice(h * hd, (h + 1) * hd)
            sum_h = leaf_part[:, at] * mine[:, heads * n + h:heads * n + h + 1]
            for i in range(n):
                sum_h = sum_h + part_recv[i, :, at].astype(jnp.float32) * mine[:, h * n + i:h * n + i + 1]
            att_own[:, at] = sum_h.astype(jnp.bfloat16)

    with scope("attag"):
        send_all("node", lambda j: att_own, att_all, a_s, a_r)
        att_all[me] = att_own[...]
        in_copies[1].wait()
        settle(others(att_all, n), a_r)

    with scope("order"):
        mixed = nn_dot(order_ref[...], att_all[...].reshape(n * own_rows, span)).astype(jnp.bfloat16)
        for h in range(heads):
            for g in range(size):
                first = (h * size + g) * hd
                lhs[:, first:first + hd] = mixed[g * branches:(g + 1) * branches, h * hd:(h + 1) * hd]

    w_copies[0].wait()
    tiles, tile = pr_own.shape[0], pr_own.shape[2]

    def mp_peer(k):
        return lax.rem(mp_hi + k, mp_halves) * 2 + mp_lo

    def project(t, carry):
        at = pl.ds(pl.multiple_of(t * tile, tile), tile)
        value = nn_dot(lhs[...], ow[:, at])
        stream[:, at] = value
        pr_own[t] = value.astype(jnp.bfloat16)
        for k in range(1, mp_halves):
            peer = mp_peer(k)
            remote(
                pr_own.at[t], pr_hi.at[mp_hi, t], h_s, h_r.at[mp_hi, t], "mp", peer
            ).start()
        return carry

    def pair(t, carry):
        at = pl.ds(pl.multiple_of(t * tile, tile), tile)
        value = stream[:, at]
        for k in range(1, mp_halves):
            peer = mp_peer(k)
            at_hi = peer // 2
            remote(
                pr_own.at[t], pr_hi.at[at_hi, t], h_s, h_r.at[at_hi, t], "mp", peer
            ).wait_recv()
            value = value + pr_hi[at_hi, t].astype(jnp.float32)
        stream[:, at] = value
        pr_pair[t] = value.astype(jnp.bfloat16)
        remote(pr_pair.at[t], pr_lo.at[t], l_s, l_r.at[t], "mp", mp_partner).start()
        return carry

    def finish(t, squares):
        at = pl.ds(pl.multiple_of(t * tile, tile), tile)
        remote(pr_pair.at[t], pr_lo.at[t], l_s, l_r.at[t], "mp", mp_partner).wait_recv()
        value = stream[:, at] + pr_lo[t].astype(jnp.float32) + res_ref[:, at].astype(jnp.float32)
        stream[:, at] = value
        xg[:, at] = (value * gain_ref[:, at]).astype(jnp.bfloat16)
        return squares + jnp.sum(value * value, axis=1, keepdims=True)

    with scope("project"):
        lax.fori_loop(0, tiles, project, 0)
    with scope("prhi"):
        in_copies[2].wait()
        in_copies[3].wait()
        lax.fori_loop(0, tiles, pair, 0)
    with scope("prlo"):
        squares = lax.fori_loop(0, tiles, finish, jnp.zeros((branches, 1), jnp.float32))

    def early_sent():
        settle(others(qall, n), q_s)
        settle(others(part_recv, n), p_s)
        settle(others(st_recv, n), t_s)
        settle(others(att_all, n), a_s)

    with scope("wwait12"):
        w_copies[1].wait()
        w_copies[2].wait()

    def turn(i):
        down = jnp.where(owner_halves - 1 - i > hi, owner_halves - 1 - i, owner_halves - 2 - i)
        up = jnp.where(i < hi, i, i + 1)
        other = jnp.where(2 * hi >= owner_halves, up, down)
        return jnp.where((i == owner_halves - 1) & (hi < owner_halves), hi, other)

    def gate_up(j, off, count):
        at = pl.ds(pl.multiple_of(j * chunk + off, 128), count)
        return nn_dot(xg[...], gw[:, at]), nn_dot(xg[...], uw[:, at])

    def gx(k, s):
        at = pl.ds(subs[s][0], subs[s][1])
        return remote(
            gx_send.at[k, :, :, at], gx_recv.at[k, :, :, at], gx_s, gx_r.at[k, s], "node", partner
        )

    def gz(k, target, slot, s):
        at = pl.ds(subs[s][0], subs[s][1])
        return remote(
            gz_send.at[k, :, :, at], gz_recv.at[slot, :, :, at], gz_s, gz_r.at[slot, s],
            "node", target * 2 + lo,
        )

    line = halves == 4 and owner_halves == 4
    outer = (hi == 0) | (hi == 3)
    beside = hi + 1 - 2 * lax.rem(hi, 2)
    across_outer = jnp.where(hi < 2, 3, 0)
    across_inner = jnp.where(hi < 2, 2, 1)
    line_turn = (
        jnp.where(outer, across_outer, beside),
        jnp.where(outer, across_inner, across_outer),
        jnp.where(outer, beside, across_inner),
        hi,
    )

    def partner_side(s, k):
        off, count = subs[s]
        gate, upward = gate_up(k * 2 + 1 - lo, off, count)
        gx_send[k, 0, :, off:off + count] = gate.astype(jnp.bfloat16)
        gx_send[k, 1, :, off:off + count] = upward.astype(jnp.bfloat16)
        gx(k, s).start()

    def own_side(s, k):
        off, count = subs[s]
        at = slice(off, off + count)
        gate, upward = gate_up(k * 2 + lo, off, count)
        gx(k, s).wait_recv()
        gate = gate + gx_recv[k, 0, :, at].astype(jnp.float32)
        upward = upward + gx_recv[k, 1, :, at].astype(jnp.float32)
        return gate, upward

    def keep_own(s, gate, upward):
        at = slice(subs[s][0], subs[s][0] + subs[s][1])
        own_sum[0, :, at] = gate
        own_sum[1, :, at] = upward

    def pass_on(s, k, target, slot, gate, upward):
        at = slice(subs[s][0], subs[s][0] + subs[s][1])
        gz_send[k, 0, :, at] = gate.astype(jnp.bfloat16)
        gz_send[k, 1, :, at] = upward.astype(jnp.bfloat16)
        gz(k, target, slot, s).start()

    def own_line(s, p):
        at = slice(subs[s][0], subs[s][0] + subs[s][1])
        k = line_turn[p]
        gate, upward = own_side(s, k)
        if p == 3:
            keep_own(s, gate, upward)
        elif p == 0:
            pass_on(s, k, beside, jnp.where(outer, 0, 2), gate, upward)
        else:
            held = p - 1

            @pl.when(outer)
            def _():
                pass_on(s, k, beside, p, gate, upward)

            @pl.when(jnp.logical_not(outer))
            def _():
                gz(k, beside, held, s).wait_recv()
                pass_on(
                    s, k, k, 3,
                    gate + gz_recv[held, 0, :, at].astype(jnp.float32),
                    upward + gz_recv[held, 1, :, at].astype(jnp.float32),
                )

    def own_direct(s, k):
        gate, upward = own_side(s, k)
        pl.when(k == hi)(lambda: keep_own(s, gate, upward))
        pl.when(k != hi)(lambda: pass_on(s, k, k, hi, gate, upward))

    def partner_turns(i, carry):
        for s in range(len(subs)):
            partner_side(s, turn(i))
        return carry

    def own_turns(i, carry):
        for s in range(len(subs)):
            own_direct(s, turn(i))
        return carry

    def act_z(k, s, owner, sem_at):
        at = pl.ds(subs[s][0], subs[s][1])
        return remote(
            act_all.at[owner, :, at], act_all.at[owner, :, at], cz_s, cz_r.at[sem_at, s],
            "node", k * 2 + lo,
        )

    def act_x(k, s, side):
        owner = k * 2 + side
        at = pl.ds(subs[s][0], subs[s][1])
        return remote(
            act_all.at[owner, :, at], act_all.at[owner, :, at], cx_s, cx_r.at[k, s], "node", partner
        )

    def other_halves(fn):
        def body(i, carry):
            down = jnp.where(halves - 1 - i > hi, halves - 1 - i, halves - 2 - i)
            fn(jnp.where(2 * hi >= halves, jnp.where(i < hi, i, i + 1), down))
            return carry

        lax.fori_loop(0, halves - 1, lambda i, carry: body(halves - 2 - i, carry), 0)

    def norm_scale():
        settle(others(sq_all, n), s_r)
        total = sq_all[0]
        for k in range(1, n):
            total = total + sq_all[k]
        mean = total / (width * n)
        sq_own_scale[...] = jnp.concatenate([lax.rsqrt(mean + norm_eps)] * 16, axis=0).T

    def owner_work(s):
        off, count = subs[s]
        at = slice(off, off + count)
        root_mean = sq_own_scale[0:branches, 0:1]

        def add(k, carry):
            return (
                carry[0] + gz_recv[k, 0, :, at].astype(jnp.float32),
                carry[1] + gz_recv[k, 1, :, at].astype(jnp.float32),
            )

        gate, upward = own_sum[0, :, at], own_sum[1, :, at]
        if line:
            for slot in (2, 3):
                gz(0, beside, slot, s).wait_recv()
                gate, upward = add(slot, (gate, upward))
        else:
            other_halves(lambda k: gz(0, k, k, s).wait_recv())
            gate, upward = lax.fori_loop(
                1, halves, lambda i, carry: add(lax.rem(hi + i, halves), carry), (gate, upward)
            )
        gate, upward = gate * root_mean, upward * root_mean
        act_all[me, :, at] = (gate / (1.0 + jnp.exp(-gate)) * upward).astype(jnp.bfloat16)
        act_x(hi, s, lo).start()
        other_halves(lambda k: act_z(k, s, me, hi).start())

    def own_act(s):
        if owners == n:
            owner_work(s)
        else:
            pl.when(me < owners)(functools.partial(owner_work, s))

    def down(owner, s):
        off, count = subs[s]
        at = pl.ds(pl.multiple_of(owner * chunk + off, 128), count)
        acc[...] += nn_dot(act_all[owner, :, off:off + count], dw[at, :])

    def forward_turns(i, carry):
        k = turn(owner_halves - 1 - i)
        for s in range(steps):
            @pl.when(k != hi)
            def _():
                act_z(k, s, k * 2 + lo, k).wait_recv()
                act_x(k, s, lo).start()

        for s in range(steps):
            down(k * 2 + lo, s)
        return carry

    def partner_acts(i, carry):
        k = turn(owner_halves - 1 - i)
        for s in range(steps):
            act_x(k, s, 1 - lo).wait_recv()
            down(k * 2 + 1 - lo, s)
        return carry

    steps = len(subs)
    acc[...] = jnp.zeros(acc.shape, jnp.float32)
    with scope("gupartner"):
        if line:
            for p in range(4):
                for s in range(steps):
                    partner_side(s, line_turn[p])
        else:
            lax.fori_loop(0, owner_halves, partner_turns, 0)
    with scope("sqsend"):
        sq_own[...] = to_lanes([squares])[0:8]
        send_all("node", lambda j: sq_own, sq_all, s_s, s_r)
        sq_all[me] = sq_own[...]
        early_sent()
    if line:
        for p in range(4):
            if p == 3:
                norm_scale()
            for s in range(steps):
                with scope(f"own{p}{s}"):
                    own_line(s, p)
    else:
        lax.fori_loop(0, owner_halves, own_turns, 0)
        norm_scale()
    w_copies[3].wait()
    for s in range(steps):
        with scope(f"act{s}"):
            own_act(s)
    with scope("forward"):
        lax.fori_loop(0, owner_halves, forward_turns, 0)
    with scope("frompartner"):
        lax.fori_loop(0, owner_halves, partner_acts, 0)

    rows_out = out_ref.shape[0]
    with scope("dnx"):
        for k in range(mp):
            dn_send[k] = acc[k * rows_out:(k + 1) * rows_out, :].astype(jnp.bfloat16)
        send_all("mp", lambda j: dn_send.at[j], dn_recv, d_s, d_r)
        dn_recv[mpi] = dn_send[mpi]
        settle(others(sq_all, n), s_s)
        for _ in range(1, mp_halves):
            settle(pr_own, h_s)
        settle(pr_pair, l_s)
        settle(gx_send, gx_s)
        settle(act_all.at[pl.ds(0, owner_halves)], cx_s)
        if owners == n:
            settle(others(gz_send, owner_halves), gz_s)
            settle(act_all.at[pl.ds(0, halves - 1)], cz_s)
        else:
            owning = hi < owner_halves
            pl.when(owning)(lambda: settle(others(gz_send, owner_halves), gz_s))
            pl.when(owning)(lambda: settle(act_all.at[pl.ds(0, halves - 1)], cz_s))
            pl.when(jnp.logical_not(owning))(lambda: settle(gz_send, gz_s))
        settle(others(dn_recv, mp), d_r)
        total = dn_recv[0].astype(jnp.float32)
        for k in range(1, mp):
            total = total + dn_recv[k].astype(jnp.float32)
        own = stream[pl.ds(pl.multiple_of(mpi * rows_out, rows_out), rows_out), :]
        out_ref[...] = (own + total).astype(jnp.bfloat16)

    with scope("drain"):
        settle(others(dn_recv, mp), d_s)


def on_device(
    n, mp,
    queries, root_keys, root_values, mid_keys, mid_values, leaf_keys, leaf_values,
    mid_length, leaf_length, branch_mid, residual, norm_gain,
    out_weight, gate_weight, up_weight, down_weight,
):
    owned, local_heads, hd = queries.shape
    heads = root_keys.shape[1]
    size = local_heads // heads
    own_rows = owned * size
    branches = owned * n
    width = residual.shape[1]
    hidden = gate_weight.shape[1]
    lane_tiles = hidden // 128
    owners = max(k for k in range(2, n + 1, 2) if lane_tiles % k == 0)
    chunk = hidden // owners
    subs, off = [], 0
    for left in range(PIECES, 0, -1):
        count = -(-(chunk - off) // (128 * left)) * 128
        if count:
            subs.append((off, count))
        off += count
    mid_slots = mid_keys.shape[1]
    leaf_slots = leaf_keys.shape[1]
    local_mids = mid_keys.shape[0]
    halves, owner_halves, mp_halves = n // 2, owners // 2, mp // 2
    group = max(1, min(n, ROWS // own_rows))
    pack = min(group, 128 // own_rows)
    tile = math.gcd(width, 256)
    tiles = width // tile

    order = np.zeros((branches * size, branches * size), np.float32)
    at = np.arange(branches * size)
    order[(at % size) * branches + at // size, at] = 1.0

    flat = [
        a.reshape(-1, hd)
        for a in (root_keys, root_values, mid_keys, mid_values, leaf_keys, leaf_values)
    ]
    kv_rows = flat[0].shape[0] + flat[2].shape[0] + flat[4].shape[0]
    span = heads * hd
    bf, f32 = jnp.bfloat16, jnp.float32
    dma = pltpu.SemaphoreType.DMA
    vmem = pl.BlockSpec(memory_space=pltpu.VMEM)
    hbm = pl.BlockSpec(memory_space=pl.ANY)
    rows_out = branches // mp
    scratch = [
        pltpu.SMEM(branch_mid.shape[:1], jnp.int32),
        pltpu.SMEM(mid_length.shape, jnp.int32),
        pltpu.SMEM(leaf_length.shape, jnp.int32),
        pltpu.VMEM((owned, local_heads, hd), bf),
        pltpu.VMEM(order.shape, bf),
        pltpu.VMEM((branches, width), bf),
        pltpu.VMEM((1, width), f32),
        pltpu.VMEM((kv_rows, span), bf),
        pltpu.VMEM((kv_rows, span), bf),
        pltpu.VMEM(out_weight.shape, bf),
        pltpu.VMEM(gate_weight.shape, bf),
        pltpu.VMEM(up_weight.shape, bf),
        pltpu.VMEM(down_weight.shape, bf),
        pltpu.VMEM((own_rows, span), bf),
        pltpu.VMEM((n, own_rows, span), bf),
        pltpu.VMEM((n, own_rows, span), bf),
        pltpu.VMEM((n, own_rows, span), bf),
        pltpu.VMEM((n // pack, 8, 128), f32),
        pltpu.VMEM((n, 8, 128), f32),
        pltpu.VMEM((own_rows, span), f32),
        pltpu.VMEM((128, 128), f32),
        pltpu.VMEM((own_rows, span), bf),
        pltpu.VMEM((n, own_rows, span), bf),
        pltpu.VMEM((branches, local_heads * hd), bf),
        pltpu.VMEM((tiles, branches, tile), bf),
        pltpu.VMEM((mp_halves, tiles, branches, tile), bf),
        pltpu.VMEM((tiles, branches, tile), bf),
        pltpu.VMEM((tiles, branches, tile), bf),
        pltpu.VMEM((branches, width), f32),
        pltpu.VMEM((8, 128), f32),
        pltpu.VMEM((n, 8, 128), f32),
        pltpu.VMEM((128, 128), f32),
        pltpu.VMEM((branches, width), bf),
        pltpu.VMEM((owner_halves, 2, branches, chunk), bf),
        pltpu.VMEM((owner_halves, 2, branches, chunk), bf),
        pltpu.VMEM((2, branches, chunk), f32),
        pltpu.VMEM((owner_halves, 2, branches, chunk), bf),
        pltpu.VMEM((halves, 2, branches, chunk), bf),
        pltpu.VMEM((owners, branches, chunk), bf),
        pltpu.VMEM((branches, width), f32),
        pltpu.VMEM((mp, rows_out, width), bf),
        pltpu.VMEM((mp, rows_out, width), bf),
        dma((7,)),
        dma((2,)),
        dma((4,)),
        dma(()),
        dma((n // group,)),
    ] + [dma(())] * 8 + [
        dma(()),
        dma((mp_halves, tiles)),
        dma(()),
        dma((tiles,)),
        dma(()),
        dma((owner_halves, len(subs))),
        dma(()),
        dma((halves, len(subs))),
        dma(()),
        dma((owner_halves, len(subs))),
        dma(()),
        dma((owner_halves, len(subs))),
        dma(()),
        dma(()),
    ]
    scale2 = hd ** -0.5 * math.log2(math.e)
    return pl.pallas_call(
        functools.partial(
            layer_kernel, n, mp, owners, scale2, local_mids, mid_slots, leaf_slots, size, subs
        ),
        out_shape=pltpu.VMEM((rows_out, width), bf),
        in_specs=[hbm] * 17,
        out_specs=vmem,
        scratch_shapes=scratch,
        compiler_params=pltpu.CompilerParams(
            collective_id=0, has_side_effects=True, vmem_limit_bytes=66900000
        ),
    )(
        branch_mid.reshape(-1), mid_length, leaf_length,
        queries, jnp.asarray(order, bf), residual, norm_gain[None, :],
        *flat, out_weight, gate_weight, up_weight, down_weight,
    )


def solution(mesh):
    in_specs = (
        P("node", "mp", None),
        P("node", "mp", None),
        P("node", "mp", None),
        P("node", None, "mp", None),
        P("node", None, "mp", None),
        P("node", None, "mp", None),
        P("node", None, "mp", None),
        P(),
        P("node"),
        P(),
        P(None, "node"),
        P("node"),
        P("mp", "node"),
        P("node", "mp"),
        P("node", "mp"),
        P("mp", "node"),
    )
    body = functools.partial(on_device, mesh.shape["node"], mesh.shape["mp"])
    return jax.shard_map(
        body, mesh=mesh, in_specs=in_specs, out_specs=P("mp", "node"), check_vma=False
    )
```
